32 devices in a mesh: dp: 8 (over z, x), fsdp: 4 (over y, core).
Axes of the slice: x: 2, y: 2, z: 4, core: 2. Of those that a mesh axis runs over, the one named last changes fastest.
Arguments:
- block_input: bfloat16 [18432, 768], P(('dp', 'fsdp')), may hold values from -6 to 6
- cotangent: bfloat16 [18432, 768], P(('dp', 'fsdp')), may hold values from -6 to 6
- time_embed: bfloat16 [32, 128], P(('dp', 'fsdp')), may hold values from -6 to 6
- ada_weight: bfloat16 [128, 4608], P('fsdp'), may hold values from -0.25 to 0.25
- ada_bias: bfloat16 [4608], P('fsdp'), may hold values from -2 to 2
- attn_gain: bfloat16 [768], P('fsdp'), may hold values from 0.5 to 1.5
- qkv_weight: bfloat16 [768, 2304], P('fsdp'), may hold values from -0.21875 to 0.21875
- out_weight: bfloat16 [768, 768], P('fsdp'), may hold values from -0.875 to 0.875
- mlp_gain: bfloat16 [768], P('fsdp'), may hold values from 0.5 to 1.5
- up_weight: bfloat16 [768, 3072], P('fsdp'), may hold values from -0.21875 to 0.21875
- up_bias: bfloat16 [3072], P('fsdp'), may hold values from -2 to 2
- down_weight: bfloat16 [3072, 768], P('fsdp'), may hold values from -0.109375 to 0.109375
- down_bias: bfloat16 [768], P('fsdp'), may hold values from -2 to 2
Outputs:
- block_output: bfloat16 [18432, 768], P(('dp', 'fsdp'))
- input_grad: float32 [18432, 768], P(('dp', 'fsdp'))
- time_grad: float32 [32, 128], P(('dp', 'fsdp'))
- ada_weight_grad: float32 [128, 4608], P('fsdp')
- ada_bias_grad: float32 [4608], P('fsdp')
- attn_gain_grad: float32 [768], P('fsdp')
- qkv_weight_grad: float32 [768, 2304], P('fsdp')
- out_weight_grad: float32 [768, 768], P('fsdp')
- mlp_gain_grad: float32 [768], P('fsdp')
- up_weight_grad: float32 [768, 3072], P('fsdp')
- up_bias_grad: float32 [3072], P('fsdp')
- down_weight_grad: float32 [3072, 768], P('fsdp')
- down_bias_grad: float32 [768], P('fsdp')
The draws below stay inside these ranges and needn't reach their ends.
All inputs are finite; a program needn't handle non-finite values.
Results may differ from the reference program's by a relative error of at most 0.015.
The reference program's roundings to bfloat16 on the way count: a program that leaves them out, or rounds other values in their place, can miss the bound.
Values may be sent and summed in bfloat16 or wider, within the bound.
No kernel may reach another device: no remote copies, remote signals or barrier semaphores. Data moves between devices by JAX's collectives and lax.ppermute only.
A program may use at most 192 MiB of HBM per device.

```python
import jax
import jax.numpy as jnp
from jax import lax

D = 768
HEADS = 12
HEAD_DIM = 64
FF = 3072
COND = 128
SEQ_LEN = 576
SEQS = 32
TOKENS = 18432


def block_levels(stream_key, extent, cuts, least, high):
    factor_of, own = 1.0, jax.random.fold_in(stream_key, 6)
    for dim, parts in cuts:
        steps = jnp.exp(jax.random.uniform(jax.random.fold_in(own, dim), (parts,), jnp.float32, least / len(cuts), high / len(cuts)))
        factor_of = factor_of * jnp.repeat(steps, extent[dim] // parts).reshape([-1 if axis == dim else 1 for axis in range(len(extent))])
    return factor_of


def noise(stream_key, extent, width, bound, shards=(), held_as=jnp.bfloat16):
    values = jax.random.normal(stream_key, extent, jnp.float32) * width
    if len(shards) > 0:
        values = block_levels(stream_key, extent, shards, -0.22, 0.18) * values
    return jnp.clip(values, min=-bound, max=bound).astype(held_as)


def setup_inputs(seed: int = 0) -> dict:
    seeds = jax.random.split(jax.random.key(seed), 14)
    block_input = noise(seeds[0], (TOKENS, D), 1.0, 6.0, ((0, 32),))
    cotangent = noise(seeds[1], (TOKENS, D), 1.0, 6.0, ((0, 32),))
    time_embed = noise(seeds[2], (SEQS, COND), 1.0, 6.0, ((0, 32),))
    ada_weight = noise(seeds[3], (COND, 6 * D), (4 * COND) ** -0.5, 0.25, ((0, 4),))
    ada_bias = noise(seeds[4], (6 * D,), 0.3, 2.0, ((0, 4),))
    attn_gain = jnp.clip(1.0 + 0.1 * jax.random.normal(seeds[5], (D,), jnp.float32), 0.5, 1.5).astype(jnp.bfloat16)
    qkv_weight = noise(seeds[6], (D, 3 * D), D ** -0.5, 0.21875, ((0, 4),))
    out_weight = noise(seeds[7], (D, D), (D // 16) ** -0.5, 0.875, ((0, 4),))
    mlp_gain = jnp.clip(1.0 + 0.1 * jax.random.normal(seeds[8], (D,), jnp.float32), 0.5, 1.5).astype(jnp.bfloat16)
    up_weight = noise(seeds[9], (D, FF), D ** -0.5, 0.21875, ((0, 4),))
    up_bias = noise(seeds[10], (FF,), 0.3, 2.0, ((0, 4),))
    down_weight = noise(seeds[11], (FF, D), FF ** -0.5, 0.109375, ((0, 4),))
    down_bias = noise(seeds[12], (D,), 0.3, 2.0, ((0, 4),))
    return dict(block_input=block_input, cotangent=cotangent, time_embed=time_embed, ada_weight=ada_weight, ada_bias=ada_bias, attn_gain=attn_gain, qkv_weight=qkv_weight, out_weight=out_weight, mlp_gain=mlp_gain, up_weight=up_weight, up_bias=up_bias, down_weight=down_weight, down_bias=down_bias)


@jax.custom_vjp
def low(v):
    return lax.optimization_barrier(v.astype(jnp.bfloat16)).astype(jnp.float32)

@jax.custom_vjp
def low_back(v):
    return v

def low_keep(v):
    return (low(v), None)

def low_pass(kept, grad):
    return (grad,)

def back_keep(v):
    return (v, None)

def back_low(kept, grad):
    return (low(grad),)
low.defvjp(low_keep, low_pass)
low_back.defvjp(back_keep, back_low)

def norm_modulate(values, gain, shift, scale):
    centre = lax.optimization_barrier(jnp.mean(values, axis=-1, keepdims=True))
    centred = values - centre
    spread = lax.optimization_barrier(jnp.mean(centred * centred, axis=-1, keepdims=True))
    return centred * lax.rsqrt(spread + 1e-05) * gain * (1.0 + scale) + shift

def rotary_tables(length, head_dim):
    half_dim = head_dim // 2
    position = jnp.arange(length).astype(jnp.float32)[:, None]
    frequency = 10000.0 ** (-2.0 * jnp.arange(half_dim).astype(jnp.float32) / head_dim)
    angles = position * frequency[None, :]
    return (jnp.cos(angles), jnp.sin(angles))

def rotate(tensor, cosines, sines):
    half_dim = tensor.shape[-1] // 2
    first = tensor[..., :half_dim]
    second = tensor[..., half_dim:]
    cos_b = cosines[:, None, :]
    sin_b = sines[:, None, :]
    return jnp.concatenate([first * cos_b - second * sin_b, second * cos_b + first * sin_b], axis=-1)

def layer(block, cond, params, cosines, sines):
    ada_weight, ada_bias, attn_gain, qkv_weight, out_weight, mlp_gain, up_weight, up_bias, down_weight, down_bias = params
    highest = lax.Precision.HIGHEST
    length = block.shape[0]
    modulation = low_back(jnp.dot(cond, ada_weight, precision=highest) + ada_bias)
    pieces = [modulation[:, index * D:(index + 1) * D] for index in range(6)]
    attn_in = low(norm_modulate(block, attn_gain, pieces[0], pieces[1]))
    qkv_proj = low_back(jnp.dot(attn_in, qkv_weight, precision=highest))
    queries = low(rotate(qkv_proj[:, :D].reshape(length, HEADS, HEAD_DIM), cosines, sines))
    keys = low(rotate(qkv_proj[:, D:2 * D].reshape(length, HEADS, HEAD_DIM), cosines, sines))
    values = low(qkv_proj[:, 2 * D:].reshape(length, HEADS, HEAD_DIM))
    scores = low_back(jnp.einsum('qhd,khd->hqk', queries, keys, precision=highest) * HEAD_DIM ** (-0.5))
    probs = low(jax.nn.softmax(scores, axis=-1))
    attended = jnp.einsum('hqk,khd->qhd', probs, values, precision=highest).reshape(length, D)
    attended = low(low_back(attended))
    attn_branch = low_back(jnp.dot(attended, out_weight, precision=highest))
    middle = block + pieces[2] * attn_branch
    mlp_in = low(norm_modulate(middle, mlp_gain, pieces[3], pieces[4]))
    pre_act = low_back(jnp.dot(mlp_in, up_weight, precision=highest) + up_bias)
    activ = low(jax.nn.gelu(pre_act, approximate=True))
    mlp_branch = low_back(jnp.dot(activ, down_weight, precision=highest) + down_bias)
    return middle + pieces[5] * mlp_branch

def reference(block_input, cotangent, time_embed, ada_weight, ada_bias, attn_gain, qkv_weight, out_weight, mlp_gain, up_weight, up_bias, down_weight, down_bias):
    cosines, sines = rotary_tables(SEQ_LEN, HEAD_DIM)
    params = tuple((item.astype(jnp.float32) for item in (ada_weight, ada_bias, attn_gain, qkv_weight, out_weight, mlp_gain, up_weight, up_bias, down_weight, down_bias)))

    def forward(block, cond, weights):
        sequences = block.reshape(SEQS, SEQ_LEN, D)
        conds = cond.reshape(SEQS, 1, COND)

        def single(pair):
            return layer(pair[0], pair[1], weights, cosines, sines)
        result = lax.map(jax.checkpoint(single), (sequences, conds))
        return result.reshape(SEQS * SEQ_LEN, D)
    output, back_fn = jax.vjp(forward, block_input.astype(jnp.float32), time_embed.astype(jnp.float32), params)
    block_grad, cond_grad, weight_grads = back_fn(cotangent.astype(jnp.float32))
    return (output.astype(jnp.bfloat16), block_grad, cond_grad, weight_grads[0], weight_grads[1], weight_grads[2], weight_grads[3], weight_grads[4], weight_grads[5], weight_grads[6], weight_grads[7], weight_grads[8], weight_grads[9])
```

```python
from functools import partial

import numpy as np

import jax
import jax.numpy as jnp
from jax import lax
from jax.experimental import pallas as pl
from jax.experimental.pallas import tpu as pltpu
from jax.sharding import PartitionSpec as P

HEAD_DIM = 64
BF = jnp.bfloat16
F32 = jnp.float32
NN = (((1,), (0,)), ((), ()))
NT = (((1,), (1,)), ((), ()))
TN = (((0,), (0,)), ((), ()))
VMEM_LIMIT = 60 * 2**20
HEADS_PER_STEP = 4
GELU_C = 0.7978845608028654
GELU_A = 0.044715


def mm(a, b, dims=NN):
    return lax.dot_general(a, b, dims, preferred_element_type=F32)


def swap(value, axis, size, bit):
    return lax.ppermute(value, axis, [(i, i ^ bit) for i in range(size)])


def bits_of(size):
    bits, bit = [], 1
    while bit < size:
        bits.append(bit)
        bit *= 2
    return bits


class Net:
    def __init__(self, mesh):
        self.dp = mesh.shape["dp"]
        self.fsdp = mesh.shape["fsdp"]
        self.d = lax.axis_index("dp")
        self.f = lax.axis_index("fsdp")
        self.core = self.f % 2
        self.row = self.f // 2
        self.side = self.d % 2

    def core_swap(self, v):
        return swap(v, "fsdp", self.fsdp, 1)

    def row_swap(self, v):
        return swap(v, "fsdp", self.fsdp, 2)

    def dp_swap(self, v, bit):
        return swap(v, "dp", self.dp, bit)


def gather_weight(net, shard):
    half = shard.shape[0] // 2
    partner = net.core_swap(shard)
    mine = lax.dynamic_slice_in_dim(shard, net.side * half, half, 0)
    near = net.row_swap(mine)
    far = net.dp_swap(near, 1)
    both = jnp.concatenate([near, far], axis=0)
    other = net.core_swap(both)
    return shard, partner, both, other


def halves(net, kept, got, bit, rows):
    half = rows // 2
    which = (net.d // bit) % 2
    cut = lambda v, w: lax.dynamic_slice_in_dim(v, w * half, half, 0).astype(F32)
    send = (cut(kept, 1 - which) + cut(got, 1 - which)).astype(BF)
    keep = (cut(kept, which) + cut(got, which)).astype(BF)
    return keep, send


def reduce_shares(net, keep, send):
    got = net.core_swap(send)
    to_row = (keep[1].astype(F32) + got[1].astype(F32)).astype(BF)
    own = (keep[0].astype(F32) + got[0].astype(F32)).astype(BF)
    got = net.row_swap(to_row)
    rows = own.shape[0]
    bits = bits_of(net.dp)
    for bit in bits[:-1]:
        own, to_send = halves(net, own, got, bit, rows)
        got = net.dp_swap(to_send, bit)
        rows //= 2
    own = (own.astype(F32) + got.astype(F32)).astype(BF)
    got = net.dp_swap(own, bits[-1])
    total = own.astype(F32) + got.astype(F32)
    for bit in reversed(bits[:-1]):
        low = total.astype(BF)
        got = net.dp_swap(low, bit)
        which = (net.d // bit) % 2
        low32, got32 = low.astype(F32), got.astype(F32)
        first = jnp.where(which == 0, low32, got32)
        second = jnp.where(which == 0, got32, low32)
        total = jnp.concatenate([first, second], axis=0)
    return total


def normed(values):
    centre = jnp.mean(values, axis=-1, keepdims=True)
    centred = values - centre
    spread = jnp.mean(centred * centred, axis=-1, keepdims=True)
    r = lax.rsqrt(spread + 1e-05)
    return centred * r, r


def norm_back(grad, n, r, gain, scale):
    e = grad * (1.0 + scale) * gain
    return r * (e - jnp.mean(e, -1, keepdims=True) - n * jnp.mean(e * n, -1, keepdims=True))


def column_sum(v):
    return jnp.sum(v, axis=0, keepdims=True)


def of_head(shape, head):
    return (lax.broadcasted_iota(jnp.int32, shape, 1) // HEAD_DIM) == head


def turn(v, cos, sin):
    half = HEAD_DIM // 2
    low = (lax.broadcasted_iota(jnp.int32, v.shape, 1) // half) % 2 == 0
    width = v.shape[1]
    other = jnp.where(low, pltpu.roll(v, width - half, 1), pltpu.roll(v, half, 1))
    return v * cos + other * sin


def place(full, pos, pieces, quarter, blocks):
    own, partner, both, other = pieces
    f, side = pos[0], pos[1]
    sub = quarter // blocks
    half = sub // 2
    width = full.shape[1]
    for k in range(blocks):
        cols = slice(k * width, (k + 1) * width)
        for ref, flip in ((own, 0), (partner, 1)):
            base = pl.multiple_of((f ^ flip) * quarter + k * sub, 16)
            full[pl.ds(base, sub), :] = ref[:, cols]
        for ref, flip in ((both, 2), (other, 3)):
            for h in range(2):
                base = pl.multiple_of((f ^ flip) * quarter + k * sub + (side ^ h) * half, 16)
                full[pl.ds(base, half), :] = ref[h * half : (h + 1) * half, cols]


def store_shares(pos, grad, keep_ref, send_ref, cols=None):
    f = pos[0]
    quarter = grad.shape[0] // 4
    for owner in range(4):
        rel = f ^ owner
        row = rel // 2
        block = grad[owner * quarter : (owner + 1) * quarter].astype(BF)

        @pl.when(rel % 2 == 0)
        def _():
            keep_ref[row] = block

        @pl.when(rel % 2 == 1)
        def _():
            send_ref[row] = block


def attention_kernel(
    pos, x_ref, gain_ref, mod_ref, w0, w1, w2, w3, cos_ref, sin_ref,
    in_ref, q_ref, k_ref, v_ref, p_ref, o_ref, full,
):
    width = x_ref.shape[1]
    step = pl.program_id(0)
    cols = q_ref.shape[1]

    @pl.when(step == 0)
    def _():
        place(full, pos, (w0, w1, w2, w3), width // 4, 1)
        n, _ = normed(x_ref[...].astype(F32))
        shift, scale = mod_ref[:, :width], mod_ref[:, width : 2 * width]
        in_ref[...] = (n * gain_ref[...] * (1.0 + scale) + shift).astype(BF)

    base = pl.multiple_of(step * cols, cols)
    attn_in = in_ref[...]
    cos, sin = cos_ref[...], sin_ref[...]
    q_all = mm(attn_in, full[:, pl.ds(base, cols)])
    k_all = mm(attn_in, full[:, pl.ds(width + base, cols)])
    v_ref[...] = mm(attn_in, full[:, pl.ds(2 * width + base, cols)]).astype(BF)
    for pair in range(cols // 128):
        sl = slice(pair * 128, pair * 128 + 128)
        q = turn(q_all[:, sl], cos, sin).astype(BF) * BF(HEAD_DIM**-0.5)
        k = turn(k_all[:, sl], cos, sin).astype(BF)
        q_ref[:, sl] = q
        k_ref[:, sl] = k
        v = v_ref[:, sl]
        outs = []
        for h in range(2):
            kh = jnp.where(of_head(k.shape, h), k, jnp.zeros_like(k))
            s = mm(kh, q, NT)
            e = jnp.exp(s - jnp.max(s, axis=0, keepdims=True))
            p = (e * (1.0 / jnp.sum(e, axis=0, keepdims=True))).astype(BF)
            p_ref[2 * pair + h] = p
            outs.append(mm(p, v, TN))
        o_ref[:, sl] = jnp.where(of_head(outs[0].shape, 0), outs[0], outs[1]).astype(BF)


def whole(shape):
    return pl.BlockSpec(shape, lambda *_: (0,) * len(shape))


def sds(shape, dtype):
    return jax.ShapeDtypeStruct(shape, dtype)


def call(body, pos, args, in_specs, outs, out_specs, grid, scratch, flops, bytes_, name):
    return pl.pallas_call(
        body,
        grid_spec=pltpu.PrefetchScalarGridSpec(
            num_scalar_prefetch=1, grid=grid, in_specs=in_specs, out_specs=out_specs, scratch_shapes=scratch
        ),
        out_shape=outs,
        compiler_params=pltpu.CompilerParams(vmem_limit_bytes=VMEM_LIMIT),
        cost_estimate=pl.CostEstimate(flops=flops, bytes_accessed=bytes_, transcendentals=0),
        name=name,
    )(pos, *args)


def attention_forward(pos, x, gain, mod, pieces, cos, sin):
    length, width = x.shape
    cols = HEADS_PER_STEP * HEAD_DIM
    heads = width // HEAD_DIM
    steps = width // cols
    row = pl.BlockSpec((length, cols), lambda j, *_: (0, j))
    return call(
        attention_kernel, pos,
        (x, gain, mod, *pieces, cos, sin),
        [whole(x.shape), whole(gain.shape), whole(mod.shape)] + [whole(p.shape) for p in pieces]
        + [whole(cos.shape), whole(sin.shape)],
        [sds(x.shape, BF)] + [sds(x.shape, BF)] * 3 + [sds((heads, length, length), BF), sds(x.shape, BF)],
        [whole(x.shape), row, row, row,
         pl.BlockSpec((HEADS_PER_STEP, length, length), lambda j, *_: (j, 0, 0)), row],
        (steps,), [pltpu.VMEM((width, 3 * width), BF)],
        2 * length * width * 3 * width + 16 * length * length * width, 20 * 2**20, "attention_forward",
    )


def middle_kernel(
    pos, o_ref, x_ref, g_ref, mod_ref, gain_ref, w0, w1, w2, w3,
    branch_ref, middle_ref, in_ref, grad_ref, full_ref,
):
    width = x_ref.shape[1]
    place(full_ref, pos, (w0, w1, w2, w3), width // 4, 1)
    piece = lambda i: mod_ref[:, i * width : (i + 1) * width]
    branch = mm(o_ref[...], full_ref[...])
    branch_ref[...] = branch
    middle = x_ref[...].astype(F32) + piece(2) * branch
    middle_ref[...] = middle
    n, _ = normed(middle)
    in_ref[...] = (n * gain_ref[...] * (1.0 + piece(4)) + piece(3)).astype(BF)
    grad_ref[...] = (piece(5) * g_ref[...].astype(F32)).astype(BF)


def middle_forward(pos, o, x, g, mod, gain, pieces):
    length, width = x.shape
    col = pieces[0].shape[1] // width - 1
    specs = [pl.BlockSpec((p.shape[0], width), lambda j, *_: (0, col)) for p in pieces]
    args = (o, x, g, mod, gain)
    return call(
        middle_kernel, pos, args + tuple(pieces), [whole(a.shape) for a in args] + specs,
        [sds(x.shape, F32), sds(x.shape, F32), sds(x.shape, BF), sds(x.shape, BF), sds((width, width), BF)],
        [whole(x.shape)] * 4 + [whole((width, width))],
        (1,), [], 2 * length * width * width, 10 * 2**20, "middle_forward",
    )


def mlp_kernel(
    start, span, first, pos, in_ref, grad_ref, bias_ref, u0, u1, u2, u3, d0, d1, d2, d3, *rest
):
    if first:
        (branch_ref, back_ref, bias_grad_ref, dd_keep, dd_send, du_keep, du_send, up, down) = rest
    else:
        (branch_in, back_in, branch_ref, back_ref, bias_grad_ref, dd_keep, dd_send, du_keep, du_send, up, down) = rest
    step = pl.program_id(0)
    width = in_ref.shape[1]

    @pl.when(step == 0)
    def _():
        place(up, pos, (u0, u1, u2, u3), width // 4, 1)
        place(down, pos, (d0, d1, d2, d3), down.shape[0] // 4, down.shape[0] // 4 // (width // 4))
        if first:
            branch_ref[...] = jnp.zeros_like(branch_ref)
            back_ref[...] = jnp.zeros_like(back_ref)
        else:
            branch_ref[...] = branch_in[...]
            back_ref[...] = back_in[...]

    quarter = down.shape[0] // 4
    base = pl.multiple_of(step * quarter + start, 128)
    mlp_in, mlp_grad = in_ref[...], grad_ref[...]
    up_t = up[:, pl.ds(base, span)]
    down_t = down[pl.ds(base, span), :]
    pre = mm(mlp_in, up_t) + bias_ref[:, pl.ds(base, span)]
    t = jnp.tanh(GELU_C * (pre + GELU_A * (pre * pre * pre)))
    activ = (0.5 * pre * (1.0 + t)).astype(BF)
    slope = 0.5 * (1.0 + t) + (0.5 * GELU_C) * pre * (1.0 - t * t) * (1.0 + (3.0 * GELU_A) * (pre * pre))
    pre_grad32 = mm(mlp_grad, down_t, NT) * slope
    pre_grad = pre_grad32.astype(BF)
    bias_grad_ref[:, pl.ds(pl.multiple_of(step * span, span), span)] = column_sum(pre_grad.astype(F32))
    branch_ref[...] += mm(activ, down_t)
    back_ref[...] += mm(pre_grad, up_t, NT)
    dd = mm(activ, mlp_grad, TN).astype(BF)
    rel = pos[0] ^ step
    row = rel // 2

    @pl.when(rel % 2 == 0)
    def _():
        dd_keep[row] = dd

    @pl.when(rel % 2 == 1)
    def _():
        dd_send[row] = dd

    store_shares(pos, mm(mlp_in, pre_grad, TN), du_keep, du_send)


def mlp(pos, mlp_in, mlp_grad, bias, ups, downs, start, span, carried):
    length, width = mlp_in.shape
    hidden = bias.shape[1]
    first = carried is None
    one = lambda p: pl.BlockSpec(p.shape, lambda *_: (0, 0), pipeline_mode=pl.Buffered(1))
    up_specs = [pl.BlockSpec((p.shape[0], hidden), lambda *_: (0, 0), pipeline_mode=pl.Buffered(1)) for p in ups]
    args = (mlp_in, mlp_grad, bias, *ups, *downs) + (() if first else carried)
    specs = [whole(a.shape) for a in args[:3]] + up_specs + [
        pl.BlockSpec((p.shape[0], hidden), lambda *_: (0, 0), pipeline_mode=pl.Buffered(1)) for p in downs
    ]
    if not first:
        specs += [one(a) for a in carried]
    acc = sds((length, width), F32)
    dd_spec = pl.BlockSpec((2, span, width), lambda *_: (0, 0, 0))
    du_spec = pl.BlockSpec((2, width // 4, span), lambda j, *_: (0, 0, j))
    return call(
        partial(mlp_kernel, start, span, first), pos, args, specs,
        [acc, acc, sds((1, 4 * span), F32)] + [sds((2, span, width), BF)] * 2 + [sds((2, width // 4, 4 * span), BF)] * 2,
        [whole((length, width))] * 2 + [whole((1, 4 * span)), dd_spec, dd_spec, du_spec, du_spec],
        (4,), [pltpu.VMEM((width, hidden), BF), pltpu.VMEM((hidden, width), BF)],
        6 * 2 * length * width * 4 * span, 20 * 2**20, "mlp_first" if first else "mlp_second",
    )


def middle_back_kernel(
    pos, back_ref, mlp_ref, middle_ref, branch_ref, g_ref, mod_ref, gain_ref, bias_ref, o_ref, out_w,
    grad_ref, out_ref, do_ref, sums_ref, keep_ref, send_ref,
):
    width = g_ref.shape[1]
    piece = lambda i: mod_ref[:, i * width : (i + 1) * width]
    g = g_ref[...].astype(F32)
    middle = middle_ref[...]
    branch = branch_ref[...]
    gain = gain_ref[...]
    mlp_branch = mlp_ref[...] + bias_ref[...]
    out_ref[...] = (middle + piece(5) * mlp_branch).astype(BF)
    n, r = normed(middle)
    back = back_ref[...]
    back_n = back * n
    back_sum = column_sum(back_n)
    grad = g + norm_back(back, n, r, gain, piece(4))
    grad_ref[...] = grad
    low = (piece(2) * grad).astype(BF)
    sums = (
        column_sum(grad * branch),
        column_sum(back),
        back_sum * gain,
        column_sum(g * mlp_branch),
        back_sum * (1.0 + piece(4)),
        column_sum((piece(5) * g).astype(BF).astype(F32)),
    )
    for i, v in enumerate(sums):
        sums_ref[:, i * width : (i + 1) * width] = v
    do_ref[...] = mm(low, out_w[...], NT).astype(BF)
    store_shares(pos, mm(o_ref[...], low, TN), keep_ref, send_ref)


def middle_back(pos, back, mlp_branch, middle, branch, g, mod, gain, bias, o, out_w):
    length, width = g.shape
    args = (back, mlp_branch, middle, branch, g, mod, gain, bias, o, out_w)
    share = sds((2, width // 4, width), BF)
    return call(
        middle_back_kernel, pos, args, [whole(a.shape) for a in args],
        [sds(g.shape, F32), sds(g.shape, BF), sds(g.shape, BF), sds((1, 6 * width), F32), share, share],
        [whole(g.shape)] * 3 + [whole((1, 6 * width)), whole(share.shape), whole(share.shape)],
        (1,), [], 4 * length * width * width, 14 * 2**20, "middle_back",
    )


def attention_back_kernel(
    pos, q_ref, k_ref, v_ref, p_ref, o_ref, do_ref, in_ref, cos_ref, sin_ref,
    grad_ref, keep_ref, send_ref,
):
    cols = q_ref.shape[1]
    cos, sin = cos_ref[...], -sin_ref[...]
    for pair in range(cols // 128):
        sl = slice(pair * 128, pair * 128 + 128)
        q, k, v, do = q_ref[:, sl], k_ref[:, sl], v_ref[:, sl], do_ref[:, sl]
        od = o_ref[:, sl].astype(F32) * do.astype(F32)
        dq, dk, dv = [], [], []
        for h in range(2):
            mask = of_head(v.shape, h)
            p = p_ref[2 * pair + h]
            dp = mm(jnp.where(mask, v, jnp.zeros_like(v)), do, NT)
            delta = jnp.sum(jnp.where(mask, od, 0.0).T, axis=0, keepdims=True)
            ds = (p.astype(F32) * (dp - delta)).astype(BF)
            dv.append(mm(p, do))
            dk.append(mm(ds, q))
            dq.append(mm(ds, k, TN))
        mask = of_head(q.shape, 0)
        both = lambda pair_: jnp.where(mask, pair_[0], pair_[1])
        grad_ref[:, sl] = turn(both(dq) * HEAD_DIM**-0.5, cos, sin).astype(BF)
        grad_ref[:, cols + pair * 128 : cols + pair * 128 + 128] = turn(both(dk), cos, sin).astype(BF)
        grad_ref[:, 2 * cols + pair * 128 : 2 * cols + pair * 128 + 128] = both(dv).astype(BF)
    store_shares(pos, mm(in_ref[...], grad_ref[...], TN), keep_ref, send_ref)


def attention_back(pos, step, q, k, v, p, o, do, attn_in, cos, sin):
    length, width = q.shape
    cols = HEADS_PER_STEP * HEAD_DIM
    row = pl.BlockSpec((length, cols), lambda *_: (0, step))
    share = sds((2, width // 4, 3 * cols), BF)
    return call(
        attention_back_kernel, pos, (q, k, v, p, o, do, attn_in, cos, sin),
        [row, row, row, pl.BlockSpec((HEADS_PER_STEP, length, length), lambda *_: (step, 0, 0)), row, row,
         whole(attn_in.shape), whole(cos.shape), whole(sin.shape)],
        [sds((length, 3 * cols), BF), share, share],
        [whole((length, 3 * cols)), whole(share.shape), whole(share.shape)],
        (1,), [], 40 * length * length * cols + 2 * length * width * 3 * cols, 8 * 2**20, "attention_back",
    )


def input_back_kernel(steps, pos, *refs):
    grads = refs[:steps]
    x_ref, mid_ref, mod_ref, gain_ref, w0, w1, w2, w3, out_ref, sums_ref, full = refs[steps:]
    width = x_ref.shape[1]
    place(full, pos, (w0, w1, w2, w3), width // 4, 1)
    cols = width // steps
    back = jnp.zeros(x_ref.shape, F32)
    for j in range(steps):
        for part in range(3):
            back += mm(
                grads[j][:, part * cols : (part + 1) * cols],
                full[:, part * width + j * cols : part * width + (j + 1) * cols], NT,
            )
    scale = mod_ref[:, width : 2 * width]
    gain = gain_ref[...]
    n, r = normed(x_ref[...].astype(F32))
    back_sum = column_sum(back * n)
    out_ref[...] = mid_ref[...] + norm_back(back, n, r, gain, scale)
    sums = (column_sum(back), back_sum * gain, back_sum * (1.0 + scale))
    for i, v in enumerate(sums):
        sums_ref[:, i * width : (i + 1) * width] = v


def input_back(pos, grads, x, mid, mod, gain, pieces):
    length, width = x.shape
    args = (*grads, x, mid, mod, gain, *pieces)
    return call(
        partial(input_back_kernel, len(grads)), pos, args, [whole(a.shape) for a in args],
        [sds(x.shape, F32), sds((1, 3 * width), F32)], [whole(x.shape), whole((1, 3 * width))],
        (1,), [pltpu.VMEM((width, 3 * width), BF)], 6 * length * width * width, 12 * 2**20, "input_back",
    )


def rotary_tables(length):
    half = HEAD_DIM // 2
    position = jnp.arange(length).astype(F32)[:, None]
    frequency = 10000.0 ** (-2.0 * jnp.arange(half).astype(F32) / HEAD_DIM)
    angles = position * frequency[None, :]
    cos, sin = jnp.cos(angles), jnp.sin(angles)
    return jnp.tile(cos, (1, 4)), jnp.concatenate([-sin, sin, -sin, sin], axis=1)


def local(
    mesh, block_input, cotangent, time_embed, ada_weight, ada_bias, attn_gain, qkv_weight, out_weight,
    mlp_gain, up_weight, up_bias, down_weight, down_bias,
):
    net = Net(mesh)
    length, width = block_input.shape
    f = net.f
    pos = jnp.stack([f, net.side]).astype(jnp.int32)
    cond = time_embed.shape[1]
    quarter = width // 4
    cos, sin = rotary_tables(length)

    small = jnp.concatenate([time_embed[0], attn_gain, mlp_gain, down_bias, up_bias, ada_bias])
    small = lax.all_gather(small, "fsdp", axis=0, tiled=False)
    qkv = gather_weight(net, qkv_weight)
    cuts = np.cumsum([0, cond, quarter, quarter, quarter, up_bias.shape[0], ada_bias.shape[0]])
    cut = lambda i: small[:, cuts[i] : cuts[i + 1]]
    flat = lambda i: cut(i).astype(F32).reshape(1, -1)
    gain_a, gain_m, bias_d, bias_u, bias_ada = (flat(i) for i in range(1, 6))
    ada_rows = ada_weight.shape[0]
    part = jnp.dot(
        lax.dynamic_slice_in_dim(cut(0), f * ada_rows, ada_rows, 1), ada_weight, preferred_element_type=F32
    )
    rows = lambda v, at, n: lax.dynamic_slice_in_dim(v, at, n, 0)
    part = rows(part, 2 * net.row, 2) + net.row_swap(rows(part, 2 * (1 - net.row), 2))
    mod = rows(part, net.core, 1) + net.core_swap(rows(part, 1 - net.core, 1)) + bias_ada

    uo = gather_weight(net, jnp.concatenate([up_weight, out_weight], axis=1))
    blocks = down_weight.shape[0] // quarter
    dn = gather_weight(
        net, jnp.concatenate([down_weight[k * quarter : (k + 1) * quarter] for k in range(blocks)], axis=1)
    )

    attn_in, q, k, v, p, o = attention_forward(pos, block_input, gain_a, mod, qkv, cos, sin)
    branch, middle, mlp_in, mlp_grad, out_full = middle_forward(
        pos, o, block_input, cotangent, mod, gain_m, uo
    )
    hidden_quarter = down_weight.shape[0]
    one = (2 * hidden_quarter) // 3
    two = hidden_quarter - one
    mb, back, bias_g1, dd_k1, dd_s1, du_k1, du_s1 = mlp(
        pos, mlp_in, mlp_grad, bias_u, uo, dn, 0, one, None
    )
    mb, back, bias_g2, dd_k2, dd_s2, du_k2, du_s2 = mlp(
        pos, mlp_in, mlp_grad, bias_u, uo, dn, one, two, (mb, back)
    )
    middle_grad, block_output, do, sums_m, ow_k, ow_s = middle_back(
        pos, back, mb, middle, branch, cotangent, mod, gain_m, bias_d, o, out_full
    )
    steps = width // (HEADS_PER_STEP * HEAD_DIM)
    backs = [attention_back(pos, j, q, k, v, p, o, do, attn_in, cos, sin) for j in range(steps)]
    input_grad, sums_a = input_back(pos, [b[0] for b in backs], block_input, middle_grad, mod, gain_a, qkv)

    d1 = reduce_shares(net, dd_k1, dd_s1)
    u1 = reduce_shares(net, du_k1, du_s1)
    d2 = reduce_shares(net, dd_k2, dd_s2)
    u2 = reduce_shares(net, du_k2, du_s2)
    ow = reduce_shares(net, ow_k, ow_s)
    qs = [reduce_shares(net, b[1], b[2]) for b in backs]

    down_grad = jnp.concatenate([d1, d2], axis=0)
    up_grad = jnp.concatenate(
        [jnp.concatenate([u1[:, i * one : (i + 1) * one], u2[:, i * two : (i + 1) * two]], axis=1) for i in range(4)],
        axis=1,
    )
    cols = HEADS_PER_STEP * HEAD_DIM
    qkv_grad = jnp.concatenate(
        [qs[j][:, part_ * cols : (part_ + 1) * cols] for part_ in range(3) for j in range(steps)], axis=1
    )

    bias_u_grad = jnp.concatenate(
        [jnp.concatenate([bias_g1[:, i * one : (i + 1) * one], bias_g2[:, i * two : (i + 1) * two]], axis=1) for i in range(4)],
        axis=1,
    )
    w = width
    row = jnp.concatenate(
        [sums_a[:, : 2 * w], sums_m[:, : 4 * w], sums_a[:, 2 * w :], sums_m[:, 4 * w :], bias_u_grad], axis=1
    ).astype(BF)
    row = jnp.concatenate([row, time_embed], axis=1)
    pair = jnp.concatenate([row, net.core_swap(row)], axis=0)
    group = jnp.concatenate([pair, net.row_swap(pair)], axis=0)
    tg = lax.dot_general(group[:, : 6 * w], ada_weight, NT, preferred_element_type=F32)
    everyone = group
    for bit in bits_of(net.dp):
        everyone = jnp.concatenate([everyone, net.dp_swap(everyone, bit)], axis=0)
    got = net.row_swap(tg[2:])
    hold = jnp.concatenate([tg[0:1], got[0:1]], axis=1)
    give = jnp.concatenate([tg[1:2], got[1:2]], axis=1)
    got = net.core_swap(give)
    parts = jnp.concatenate(
        [hold[:, :ada_rows], got[:, :ada_rows], hold[:, ada_rows:], got[:, ada_rows:]], axis=0
    )
    time_grad = jnp.take(parts, jnp.arange(4) ^ f, axis=0).reshape(1, cond)

    mod_all = everyone[:, : 6 * w]
    te_all = lax.dynamic_slice_in_dim(everyone[:, -cond:], f * ada_rows, ada_rows, 1)
    ada_weight_grad = lax.dot_general(te_all, mod_all, TN, preferred_element_type=F32)
    own_cols = lambda start, size: jnp.sum(
        lax.dynamic_slice_in_dim(everyone[:, start : start + 4 * size], f * size, size, 1).astype(F32), axis=0
    )
    ada_bias_grad = own_cols(0, 6 * w // 4)
    attn_gain_grad = own_cols(6 * w, quarter)
    mlp_gain_grad = own_cols(7 * w, quarter)
    down_bias_grad = own_cols(8 * w, quarter)
    up_bias_grad = own_cols(9 * w, up_bias.shape[0])
    return (
        block_output, input_grad, time_grad, ada_weight_grad, ada_bias_grad, attn_gain_grad, qkv_grad, ow,
        mlp_gain_grad, up_grad, up_bias_grad, down_grad, down_bias_grad,
    )


def solution(mesh):
    rows, shard, line = P(("dp", "fsdp"), None), P("fsdp", None), P("fsdp")
    return jax.shard_map(
        partial(local, mesh),
        mesh=mesh,
        in_specs=(rows, rows, rows, shard, line, line, shard, shard, line, shard, line, shard, line),
        out_specs=(rows, rows, rows, shard, line, line, shard, shard, line, shard, line, shard, line),
        check_vma=False,
    )
```

```python
from functools import partial

import numpy as np

import jax
import jax.numpy as jnp
from jax import lax
from jax.experimental import pallas as pl
from jax.experimental.pallas import tpu as pltpu
from jax.sharding import PartitionSpec as P

HEAD_DIM = 64
BF = jnp.bfloat16
F32 = jnp.float32
NN = (((1,), (0,)), ((), ()))
NT = (((1,), (1,)), ((), ()))
TN = (((0,), (0,)), ((), ()))
VMEM_LIMIT = 60 * 2**20
HEADS_PER_STEP = 4
GELU_C = 0.7978845608028654
GELU_A = 0.044715


def mm(a, b, dims=NN):
    return lax.dot_general(a, b, dims, preferred_element_type=F32)


UNIT = 64


def swap(value, axis, size, bit):
    return lax.ppermute(value, axis, [(i, i ^ bit) for i in range(size)])


def bits_of(size):
    bits, bit = [], 1
    while bit < size:
        bits.append(bit)
        bit *= 2
    return bits


def tie(*values):
    return lax.optimization_barrier(values)


class Net:
    def __init__(self, mesh):
        self.dp = mesh.shape["dp"]
        self.fsdp = mesh.shape["fsdp"]
        self.d = lax.axis_index("dp")
        self.f = lax.axis_index("fsdp")
        self.core = self.f % 2
        self.row = self.f // 2
        self.side = self.d % 2
        self.zero = self.d // self.dp

    def core_swap(self, v):
        return swap(v, "fsdp", self.fsdp, 1)

    def row_swap(self, v):
        return swap(v, "fsdp", self.fsdp, 2)

    def dp_swap(self, v, bit):
        return swap(v, "dp", self.dp, bit)


def follow(after, *values):
    if after is None:
        return list(values)
    return list(tie(after, *values)[1:])


class Part:
    def __init__(self, base, cuts=()):
        self.base, self.cuts = base, cuts

    def cut(self, which):
        return Part(self.base, self.cuts + (which,))

    def read(self):
        v = self.base
        for which in self.cuts:
            half = v.shape[0] // 2
            v = lax.dynamic_slice_in_dim(v, which * half, half, 0)
        return v.astype(F32)


def add(parts):
    return sum(p.read() for p in parts).astype(BF)


def hold(after, parts):
    bases = []
    for p in parts:
        if not any(p.base is b for b in bases):
            bases.append(p.base)
    held = follow(after, *bases)
    return [Part(next(h for h, b in zip(held, bases) if b is p.base), p.cuts) for p in parts]


def chunk_steps(net, keep, send, row_first, extend):
    got, after = yield ("core", send)
    kept = Part(*follow(after, keep))
    came = Part(got)
    near, far = [kept.cut(net.zero), came.cut(net.zero)], [kept.cut(1 + net.zero), came.cut(1 + net.zero)]
    bits = bits_of(net.dp)
    todo = (["row"] + bits[:-1]) if row_first else (bits[:1] + ["row"] + bits[1:-1])
    split = True
    for where in todo:
        if where == "row":
            got, after = yield (where, add(far))
            near = hold(after, near) + [Part(got)]
            split = False
            if extend:
                near = [Part(extend(near, after))]
            continue
        which = (net.d // where) % 2
        give = lambda parts: add([p.cut(1 - which) for p in parts])
        stay = lambda parts: [p.cut(which) for p in parts]
        if split:
            (near_got, far_got), after = yield (where, tie(give(near), give(far)))
            both = hold(after, near + far)
            near, far = stay(both[: len(near)]) + [Part(near_got)], stay(both[len(near) :]) + [Part(far_got)]
        else:
            got, after = yield (where, give(near))
            near = stay(hold(after, near)) + [Part(got)]
    own = add(near)
    got, after = yield (bits[-1], own)
    total = add(hold(after, [Part(own)]) + [Part(got)])
    for bit in reversed(bits[:-1]):
        got, after = yield (bit, total)
        if bit != 1:
            first = (net.d // bit) % 2 == 0
            (total,) = follow(after, total)
            total = jnp.concatenate([jnp.where(first, total, got), jnp.where(first, got, total)], axis=0)
    yield ("end", (total, got))


class Chunk:
    def __init__(self, net, shares, row_first=True, extend=None):
        self.net = net
        self.steps = chunk_steps(net, *shares, row_first, extend)
        self.where, self.ready = next(self.steps)
        self.got = net.core_swap(self.ready)

    def step(self, after):
        self.where, self.ready = self.steps.send((self.got, after))
        if self.where == "end":
            return after
        if self.where == "row":
            self.got = self.net.row_swap(self.ready)
        elif isinstance(self.ready, (list, tuple)):
            self.got = [self.net.dp_swap(v, self.where) for v in self.ready]
            return self.ready[0]
        else:
            self.got = self.net.dp_swap(self.ready, self.where)
        return self.ready


def normed(values):
    centre = jnp.mean(values, axis=-1, keepdims=True)
    centred = values - centre
    spread = jnp.mean(centred * centred, axis=-1, keepdims=True)
    r = lax.rsqrt(spread + 1e-05)
    return centred * r, r


def norm_back(grad, n, r, gain, scale):
    e = grad * (1.0 + scale) * gain
    return r * (e - jnp.mean(e, -1, keepdims=True) - n * jnp.mean(e * n, -1, keepdims=True))


def column_sum(v):
    return jnp.sum(v, axis=0, keepdims=True)


def of_head(shape, head):
    return (lax.broadcasted_iota(jnp.int32, shape, 1) // HEAD_DIM) == head


def turn(v, cos, sin):
    half = HEAD_DIM // 2
    low = (lax.broadcasted_iota(jnp.int32, v.shape, 1) // half) % 2 == 0
    width = v.shape[1]
    other = jnp.where(low, pltpu.roll(v, width - half, 1), pltpu.roll(v, half, 1))
    return v * cos + other * sin


def place_near(full, pos, own, partner, cols=((0, 0, None),)):
    rows = own.shape[0]
    for ref, flip in ((own, 0), (partner, 1)):
        base = pl.multiple_of((pos[0] ^ flip) * rows, UNIT)
        for to, at, width in cols:
            width = width or full.shape[1]
            full[pl.ds(base, rows), to : to + width] = ref[:, at : at + width]


def place_far(full, pos, far, rows, at, width):
    half = UNIT // 2
    for i, ref in enumerate(far):
        for k in range(rows // UNIT):
            base = pl.multiple_of((pos[0] ^ (2 + i // 2)) * rows + k * UNIT + (pos[1] ^ (i % 2)) * half, half)
            full[pl.ds(base, half), :] = ref[:, at + k * width : at + (k + 1) * width]


def store_shares(pos, grad, shares, at):
    quarter, width = grad.shape[0] // 4, grad.shape[1]
    for owner in range(4):
        rel = pos[0] ^ owner
        blocks = [
            grad[owner * quarter + k * UNIT : owner * quarter + (k + 1) * UNIT].astype(BF)
            for k in range(quarter // UNIT)
        ]
        put_shares(rel, blocks, shares, at)


def put_shares(rel, blocks, shares, at):
    def put(ref, row):
        for k, block in enumerate(blocks):
            ref[row : row + UNIT, at(k, block.shape[1])] = block

    for index in range(4):
        pl.when(rel == index)(partial(put, shares[index % 2], index // 2 * UNIT))


def pack_kernel(plan, pos, *refs):
    half = UNIT // 2
    outs = refs[len(refs) - len(plan) :]
    for out, moves in zip(outs, plan):
        to = 0
        for src, row, col, width in moves:
            base = pl.multiple_of(row + pos[1] * half, half)
            out[:, to : to + width] = refs[src][pl.ds(base, half), col : col + width]
            to += width


def pack_halves(pos, plan, arrays):
    outs = [sds((UNIT // 2, sum(m[3] for m in moves)), BF) for moves in plan]
    return call(
        partial(pack_kernel, plan), pos, arrays, [once(a.shape) for a in arrays], outs, [once(o.shape) for o in outs],
        (1,), [], "pack_halves",
    )


def attention_kernel(group, first, pos, x_ref, gain_ref, mod_ref, own, partner, n0, n1, n2, n3, cos_ref, sin_ref, *rest):
    if first:
        in_ref, q_ref, k_ref, v_ref, p_ref, o_ref, full = rest
    else:
        q_ref, k_ref, v_ref, p_ref, o_ref, full = rest
        in_ref = x_ref
    cols = q_ref.shape[1]
    step = pl.program_id(0)
    width = x_ref.shape[1]

    @pl.when(step == 0)
    def _():
        place_groups(full, pos, own, partner, (n0, n1, n2, n3), group, cols)
        if first:
            n, _ = normed(x_ref[...].astype(F32))
            shift, scale = mod_ref[:, :width], mod_ref[:, width : 2 * width]
            in_ref[...] = (n * gain_ref[...] * (1.0 + scale) + shift).astype(BF)

    base = pl.multiple_of(step * 3 * cols, cols)
    attn_in = in_ref[...]
    cos, sin = cos_ref[...], sin_ref[...]
    q_all = mm(attn_in, full[:, pl.ds(base, cols)])
    k_all = mm(attn_in, full[:, pl.ds(base + cols, cols)])
    v_ref[...] = mm(attn_in, full[:, pl.ds(base + 2 * cols, cols)]).astype(BF)
    for pair in range(cols // 128):
        sl = slice(pair * 128, pair * 128 + 128)
        q = turn(q_all[:, sl], cos, sin).astype(BF) * BF(HEAD_DIM**-0.5)
        k = turn(k_all[:, sl], cos, sin).astype(BF)
        q_ref[:, sl] = q
        k_ref[:, sl] = k
        v = v_ref[:, sl]
        outs = []
        for h in range(2):
            kh = jnp.where(of_head(k.shape, h), k, jnp.zeros_like(k))
            s = mm(kh, q, NT)
            e = jnp.exp(s - jnp.max(s, axis=0, keepdims=True))
            p = (e * (1.0 / jnp.sum(e, axis=0, keepdims=True))).astype(BF)
            p_ref[2 * pair + h] = p
            outs.append(mm(p, v, TN))
        o_ref[:, sl] = jnp.where(of_head(outs[0].shape, 0), outs[0], outs[1]).astype(BF)


def whole(shape):
    return pl.BlockSpec(shape, lambda *_: (0,) * len(shape))


def once(shape):
    return pl.BlockSpec(shape, lambda *_: (0,) * len(shape), pipeline_mode=pl.Buffered(1))


def place_groups(full, pos, own, partner, far, group, cols):
    width = own.shape[1] // 3
    moves = [
        ((3 * j + part) * cols, part * width + (group + j) * cols, cols)
        for j in range(full.shape[1] // (3 * cols)) for part in range(3)
    ]
    place_near(full, pos, own, partner, moves)
    place_far(full, pos, far, own.shape[0], 0, full.shape[1])


def sds(shape, dtype):
    return jax.ShapeDtypeStruct(shape, dtype)


def call(body, pos, args, in_specs, outs, out_specs, grid, scratch, name, after=None, cost=0, aliases={}):
    if after is not None:
        inner, afters = body, after if isinstance(after, tuple) else (after,)
        body = lambda pos_ref, *refs: inner(pos_ref, *refs[len(afters) :])
        args, in_specs = (*afters, *args), [pl.BlockSpec(memory_space=pl.ANY)] * len(afters) + [*in_specs]
    return pl.pallas_call(
        body,
        grid_spec=pltpu.PrefetchScalarGridSpec(
            num_scalar_prefetch=1, grid=grid, in_specs=in_specs, out_specs=out_specs, scratch_shapes=scratch
        ),
        out_shape=outs,
        compiler_params=pltpu.CompilerParams(vmem_limit_bytes=VMEM_LIMIT),
        cost_estimate=pl.CostEstimate(flops=1024 + cost * 10**9, bytes_accessed=1024, transcendentals=0),
        input_output_aliases=aliases,
        name=name,
    )(pos, *args)


def attention_forward(pos, group, count, first, x, gain, mod, pieces, cos, sin):
    length, width = x.shape
    cols = HEADS_PER_STEP * HEAD_DIM
    row = pl.BlockSpec((length, cols), lambda j, *_: (0, j))
    args = (x, gain, mod, *pieces, cos, sin)
    qkv_out = sds((length, count * cols), BF)
    outs = [qkv_out] * 3 + [sds((count * HEADS_PER_STEP, length, length), BF), qkv_out]
    specs = [row, row, row, pl.BlockSpec((HEADS_PER_STEP, length, length), lambda j, *_: (j, 0, 0)), row]
    if first:
        outs, specs = [sds(x.shape, BF)] + outs, [whole(x.shape)] + specs
    return call(
        partial(attention_kernel, group, first), pos, args, [once(a.shape) for a in args], outs, specs,
        (count,), [pltpu.VMEM((width, count * 3 * cols), BF)], "attention_forward", cost=30,
    )


ROWS = 192


def rows_of(shape):
    return pl.BlockSpec((ROWS, shape[1]), lambda i, *_: (i, 0))


def middle_kernel(count, units, pos, *refs):
    o_refs, refs = refs[:count], refs[count:]
    x_ref, g_ref, mod_ref, gain_ref, own, partner, *far = refs[: 6 + 4 * units]
    branch_ref, middle_ref, in_ref, grad_ref, full = refs[6 + 4 * units :]
    width = x_ref.shape[1]
    half = UNIT // 2

    @pl.when(pl.program_id(0) == 0)
    def _():
        place_near(full, pos, own, partner)
        for i in range(4):
            for k in range(units):
                base = (pos[0] ^ (2 + i // 2)) * own.shape[0] + k * UNIT + (pos[1] ^ (i % 2)) * half
                full[pl.ds(pl.multiple_of(base, half), half), :] = far[i * units + k][...]

    piece = lambda i: mod_ref[:, i * width : (i + 1) * width]
    branch, at = jnp.zeros(x_ref.shape, F32), 0
    for o_ref in o_refs:
        branch += mm(o_ref[...], full[at : at + o_ref.shape[1], :])
        at += o_ref.shape[1]
    branch_ref[...] = branch
    middle = x_ref[...].astype(F32) + piece(2) * branch
    middle_ref[...] = middle
    n, _ = normed(middle)
    in_ref[...] = (n * gain_ref[...] * (1.0 + piece(4)) + piece(3)).astype(BF)
    grad_ref[...] = (piece(5) * g_ref[...].astype(F32)).astype(BF)


def middle_forward(pos, os, x, g, mod, gain, own, partner, far, at):
    length, width = x.shape
    units = own.shape[0] // UNIT
    args = (*os, x, g, mod, gain, own, partner, *[p for p in far for _ in range(units)])
    specs = [rows_of(a.shape) for a in (*os, x, g)] + [once(a.shape) for a in (mod, gain, own, partner)]
    specs += [
        pl.BlockSpec((UNIT // 2, width), lambda *_, k=k: (0, at // width + k), pipeline_mode=pl.Buffered(1))
        for _ in far for k in range(units)
    ]
    full = sds((width, width), BF)
    return call(
        partial(middle_kernel, len(os), units), pos, args, specs,
        [sds(x.shape, F32), sds(x.shape, F32), sds(x.shape, BF), sds(x.shape, BF), full],
        [rows_of(x.shape)] * 4 + [whole(full.shape)], (length // ROWS,), [], "middle_forward", cost=30,
    )


TILE = 256


def mlp_kernel(start, span, first, joint, down_at, pos, *refs):
    tiles = span // TILE
    refs = list(refs)
    take = lambda n: [refs.pop(0) for _ in range(n)]
    in_ref, grad_ref, bias_ref = take(3)
    own_up, partner_up = take(tiles), take(tiles)
    units = own_up[0].shape[0] // UNIT
    far_up = [take(units) for _ in range(4)]
    own_down, partner_down, *far_down = take(6)
    if not first:
        branch_in, back_in = take(2)
    branch_ref, back_ref, bias_grad_ref = take(3)
    shares_d = take(2)
    shares_u = shares_d if joint else take(2)
    up, down = refs
    step = pl.program_id(0)
    hidden = 4 * own_down.shape[0]
    rows = own_up[0].shape[0]
    half = UNIT // 2
    f, side = pos[0], pos[1]

    @pl.when(step == 0)
    def _():
        if first:
            branch_ref[...] = jnp.zeros_like(branch_ref)
            back_ref[...] = jnp.zeros_like(back_ref)
        else:
            branch_ref[...] = branch_in[...]
            back_ref[...] = back_in[...]

    for many, flip in ((own_up, 0), (partner_up, 1)):
        base = pl.multiple_of((f ^ flip) * rows, UNIT)
        for i, ref in enumerate(many):
            up[pl.ds(base, rows), i * TILE : (i + 1) * TILE] = ref[...]
    for i, many in enumerate(far_up):
        for k, ref in enumerate(many):
            base = pl.multiple_of((f ^ (2 + i // 2)) * rows + k * UNIT + (side ^ (i % 2)) * half, half)
            up[pl.ds(base, half), :] = ref[...]

    rel = f ^ step
    width = in_ref.shape[1]
    for index, ref in ((0, own_down), (1, partner_down)):

        @pl.when(rel == index)
        def _():
            down[...] = ref[start : start + span, :]

    for index, pair in ((2, far_down[:2]), (3, far_down[2:])):

        @pl.when(rel == index)
        def _():
            for h, ref in enumerate(pair):
                for k in range(span // UNIT):
                    base = pl.multiple_of(k * UNIT + (side ^ h) * half, half)
                    down[pl.ds(base, half), :] = ref[:, down_at + k * width : down_at + (k + 1) * width]

    mlp_in, mlp_grad = in_ref[...], grad_ref[...]
    up_t, down_t = up[...], down[...]
    base = pl.multiple_of(step * (hidden // 4) + start, 128)
    pre = mm(mlp_in, up_t) + bias_ref[:, pl.ds(base, span)]
    t = jnp.tanh(GELU_C * (pre + GELU_A * (pre * pre * pre)))
    activ = (0.5 * pre * (1.0 + t)).astype(BF)
    slope = 0.5 * (1.0 + t) + (0.5 * GELU_C) * pre * (1.0 - t * t) * (1.0 + (3.0 * GELU_A) * (pre * pre))
    pre_grad = (mm(mlp_grad, down_t, NT) * slope).astype(BF)
    bias_grad_ref[:, pl.ds(pl.multiple_of(step * span, span), span)] = column_sum(pre_grad.astype(F32))
    branch_ref[...] += mm(activ, down_t)
    back_ref[...] += mm(pre_grad, up_t, NT)
    dd = mm(activ, mlp_grad, TN).astype(BF)
    put_shares(rel, [dd[k * UNIT : (k + 1) * UNIT] for k in range(span // UNIT)], shares_d, lambda k, w: slice(k * w, (k + 1) * w))
    after = (span // UNIT) * width if joint else 0
    at = lambda k, w: pl.ds(pl.multiple_of(after + (step * units + k) * w, 128), w)
    store_shares(pos, mm(mlp_in, pre_grad, TN), shares_u, at)


def mlp(pos, mlp_in, mlp_grad, bias, ups, downs, down_at, start, span, carried, joint, after=None):
    length, width = mlp_in.shape
    first = carried is None
    rows, hidden = ups[0].shape
    tiles, units, per = span // TILE, rows // UNIT, hidden // 4 // TILE
    args = [mlp_in, mlp_grad, bias]
    specs = [once(a.shape) for a in args]
    for ref in ups[:2]:
        for i in range(tiles):
            args.append(ref)
            specs.append(pl.BlockSpec((rows, TILE), lambda s, *_, i=i: (0, s * per + start // TILE + i)))
    for ref in ups[2:]:
        for k in range(units):
            args.append(ref)
            specs.append(pl.BlockSpec((UNIT // 2, span), lambda s, *_, k=k: (0, k * 4 + s)))
    args += list(downs)
    specs += [once(a.shape) for a in downs]
    if not first:
        args += list(carried)
        specs += [once(a.shape) for a in carried]
    acc = sds((length, width), F32)
    cols_d, cols_u = (span // UNIT) * width, 4 * units * span
    shares = [sds((2 * UNIT, c), BF) for c in ((cols_d + cols_u,) if joint else (cols_d, cols_u)) for _ in range(2)]
    return call(
        partial(mlp_kernel, start, span, first, joint, down_at), pos, args, specs,
        [acc, acc, sds((1, 4 * span), F32), *shares],
        [once((length, width))] * 2 + [once((1, 4 * span))] + [once(v.shape) for v in shares],
        (4,), [pltpu.VMEM((width, span), BF), pltpu.VMEM((span, width), BF)], "mlp_first" if first else "mlp_second", after,
        60 if first else 0,
    )


def add_sums(ref, sums):
    @pl.when(pl.program_id(0) == 0)
    def _():
        ref[...] = jnp.zeros_like(ref)

    for i, v in enumerate(sums):
        width = v.shape[1]
        ref[:, i * width : (i + 1) * width] += v


def middle_back_kernel(
    pos, back_ref, mlp_ref, middle_ref, branch_ref, g_ref, mod_ref, gain_ref, bias_ref, out_w,
    grad_ref, out_ref, low_ref, do_ref, sums_ref,
):
    width = g_ref.shape[1]
    piece = lambda i: mod_ref[:, i * width : (i + 1) * width]
    g = g_ref[...].astype(F32)
    middle = middle_ref[...]
    branch = branch_ref[...]
    gain = gain_ref[...]
    mlp_branch = mlp_ref[...] + bias_ref[...]
    out_ref[...] = (middle + piece(5) * mlp_branch).astype(BF)
    n, r = normed(middle)
    back = back_ref[...]
    back_sum = column_sum(back * n)
    grad = g + norm_back(back, n, r, gain, piece(4))
    grad_ref[...] = grad
    low = (piece(2) * grad).astype(BF)
    low_ref[...] = low
    sums = (
        column_sum(grad * branch),
        column_sum(back),
        back_sum * gain,
        column_sum(g * mlp_branch),
        back_sum * (1.0 + piece(4)),
        column_sum((piece(5) * g).astype(BF).astype(F32)),
    )
    add_sums(sums_ref, sums)
    do_ref[...] = mm(low, out_w[...], NT).astype(BF)


def middle_back(pos, back, mlp_branch, middle, branch, g, mod, gain, bias, out_w, after):
    length, width = g.shape
    args = (back, mlp_branch, middle, branch, g, mod, gain, bias, out_w)
    return call(
        middle_back_kernel, pos, args, [rows_of(a.shape) for a in args[:5]] + [once(a.shape) for a in args[5:]],
        [sds(g.shape, F32), sds(g.shape, BF), sds(g.shape, BF), sds(g.shape, BF), sds((1, 6 * width), F32)],
        [rows_of(g.shape)] * 4 + [whole((1, 6 * width))], (length // ROWS,), [], "middle_back", after, 60,
    )


def attention_back_kernel(extra, groups, pos, q_ref, k_ref, v_ref, p_ref, o_ref, do_ref, in_ref, cos_ref, sin_ref, *rest):
    rest = list(rest)
    if extra:
        o_all = [rest.pop(0) for _ in range(extra)]
        low_ref = rest.pop(0)
    grad_ref, *shares = rest
    cols = q_ref.shape[1]
    at = lambda k, w: slice(k * w, (k + 1) * w)

    def heads():
        cos, sin = cos_ref[...], -sin_ref[...]
        for pair in range(cols // 128):
            sl = slice(pair * 128, pair * 128 + 128)
            q, k, v, do = q_ref[:, sl], k_ref[:, sl], v_ref[:, sl], do_ref[:, sl]
            od = o_ref[:, sl].astype(F32) * do.astype(F32)
            dq, dk, dv = [], [], []
            for h in range(2):
                mask = of_head(v.shape, h)
                p = p_ref[2 * pair + h]
                dp = mm(jnp.where(mask, v, jnp.zeros_like(v)), do, NT)
                delta = jnp.sum(jnp.where(mask, od, 0.0).T, axis=0, keepdims=True)
                ds = (p.astype(F32) * (dp - delta)).astype(BF)
                dv.append(mm(p, do))
                dk.append(mm(ds, q))
                dq.append(mm(ds, k, TN))
            mask = of_head(q.shape, 0)
            both = lambda pair_: jnp.where(mask, pair_[0], pair_[1])
            grad_ref[:, sl] = turn(both(dq) * HEAD_DIM**-0.5, cos, sin).astype(BF)
            grad_ref[:, cols + pair * 128 : cols + pair * 128 + 128] = turn(both(dk), cos, sin).astype(BF)
            grad_ref[:, 2 * cols + pair * 128 : 2 * cols + pair * 128 + 128] = both(dv).astype(BF)
        store_shares(pos, mm(in_ref[...], grad_ref[...], TN), shares, at)

    if not extra:
        heads()
        return
    step = pl.program_id(0)
    pl.when(step < groups)(heads)

    @pl.when(step == groups)
    def _():
        low = low_ref[...]
        parts = [mm(o_[...], low, TN) for o_ in o_all]
        store_shares(pos, jnp.concatenate(parts, axis=0), shares, at)


def attention_back(pos, saved, do, do_at, attn_in, cos, sin, extra, after):
    q, k, v, p, o = saved
    length, width = attn_in.shape
    cols = HEADS_PER_STEP * HEAD_DIM
    groups = q.shape[1] // cols
    last = groups - 1
    row = pl.BlockSpec((length, cols), lambda j, *_: (0, jnp.minimum(j, last)))
    do_row = pl.BlockSpec((length, cols), lambda j, *_: (0, do_at // cols + jnp.minimum(j, last)))
    steps = groups + (1 if extra else 0)
    share = sds((2 * UNIT, steps * width // 4 // UNIT * 3 * cols), BF)
    share_spec = pl.BlockSpec((2 * UNIT, width // 4 // UNIT * 3 * cols), lambda j, *_: (0, j))
    args = [q, k, v, p, o, do, attn_in, cos, sin]
    specs = [row, row, row, pl.BlockSpec((HEADS_PER_STEP, length, length), lambda j, *_: (jnp.minimum(j, last), 0, 0)),
             row, do_row, once(attn_in.shape), once(cos.shape), once(sin.shape)]
    if extra:
        args += [*extra[0], extra[1]]
        specs += [once(a.shape) for a in (*extra[0], extra[1])]
    return call(
        partial(attention_back_kernel, len(extra[0]) if extra else 0, groups), pos, args, specs,
        [sds((length, 3 * groups * cols), BF)] + [share] * 2,
        [pl.BlockSpec((length, 3 * cols), lambda j, *_: (0, jnp.minimum(j, last)))] + [share_spec] * 2,
        (steps,), [], "attention_back", after,
    )


def input_back_kernel(starts, count, pos, *refs):
    grads, refs = refs[: len(starts)], refs[len(starts) :]
    own, partner, *far = refs[: 2 + 4 * len(starts)]
    x_ref, mid_ref, mod_ref, gain_ref, sums_m, te, *rest = refs[2 + 4 * len(starts) :]
    biases, (out_ref, row_ref, sums_ref, *fulls) = rest[:count], rest[count:]
    width = x_ref.shape[1]
    cols = HEADS_PER_STEP * HEAD_DIM

    @pl.when(pl.program_id(0) == 0)
    def _():
        for i, full in enumerate(fulls):
            place_groups(full, pos, own, partner, far[4 * i : 4 * i + 4], starts[i], cols)

    back = jnp.zeros(x_ref.shape, F32)
    for grad, full in zip(grads, fulls):
        back += mm(grad[...], full[...], NT)
    scale = mod_ref[:, width : 2 * width]
    gain = gain_ref[...]
    n, r = normed(x_ref[...].astype(F32))
    back_sum = column_sum(back * n)
    out_ref[...] = mid_ref[...] + norm_back(back, n, r, gain, scale)
    add_sums(sums_ref, (column_sum(back), back_sum * gain, back_sum * (1.0 + scale)))

    @pl.when(pl.program_id(0) == pl.num_programs(0) - 1)
    def _():
        w = width
        row_ref[:, : 2 * w] = sums_ref[:, : 2 * w].astype(BF)
        row_ref[:, 2 * w : 6 * w] = sums_m[:, : 4 * w].astype(BF)
        row_ref[:, 6 * w : 7 * w] = sums_ref[:, 2 * w :].astype(BF)
        row_ref[:, 7 * w : 9 * w] = sums_m[:, 4 * w :].astype(BF)
        at = 9 * w
        spans = [b.shape[1] // 4 for b in biases]
        for i in range(4):
            for b, span in zip(biases, spans):
                row_ref[:, at : at + span] = b[:, i * span : (i + 1) * span].astype(BF)
                at += span
        row_ref[:, at:] = te[...]


def input_back(pos, grads, starts, weights, x, mid, mod, gain, sums_m, te, biases, after):
    length, width = x.shape
    args = (*grads, *weights, x, mid, mod, gain, sums_m, te, *biases)
    split = {*range(len(grads))} | {len(grads) + len(weights), len(grads) + len(weights) + 1}
    specs = [rows_of(a.shape) if i in split else once(a.shape) for i, a in enumerate(args)]
    row = (1, 9 * width + sum(b.shape[1] for b in biases) + te.shape[1])
    return call(
        partial(input_back_kernel, starts, len(biases)), pos, args, specs,
        [sds(x.shape, F32), sds(row, BF)], [rows_of(x.shape), whole(row)], (length // ROWS,),
        [pltpu.VMEM((1, 3 * width), F32)] + [pltpu.VMEM((width, g.shape[1]), BF) for g in grads], "input_back", after,
    )


SMALL = 256


def ada_kernel(count, pos, pair, got, shard, *refs):
    parts, (sums_ref, keep_ref, send_ref, all_rows) = refs[:count], refs[count:]
    rows, width = shard.shape
    cond = 4 * rows
    at = parts[0].shape[1]
    fold = UNIT // rows
    te_at = pair.shape[1] - cond
    all_rows[0:2, :] = pair[...].astype(F32)
    all_rows[2:4, :] = got[...].astype(F32)
    sums_ref[:, :at] = sum(p[:UNIT, :].astype(F32) for p in parts).astype(BF)
    mods = all_rows[0:4, :width].astype(BF)
    te = all_rows[0:4, te_at:].astype(BF)
    lane = lax.broadcasted_iota(jnp.int32, (rows, cond), 1)
    pick = (lane == pos[0] * rows + lax.broadcasted_iota(jnp.int32, (rows, cond), 0)).astype(BF)
    te_own = mm(pick, te, NT).astype(BF)
    grad = mm(te_own, mods).astype(BF)
    part = width // fold
    for i in range(fold):
        sums_ref[i * rows : (i + 1) * rows, at : at + part] = grad[:, i * part : (i + 1) * part]
    at += part
    total = jnp.sum(all_rows[0:4, :te_at], axis=0, keepdims=True)
    sums_ref[:, at:] = jnp.zeros((UNIT, SMALL), BF)
    for i in range(te_at // SMALL):
        sums_ref[i : i + 1, at : at + SMALL] = total[:, i * SMALL : (i + 1) * SMALL].astype(BF)
    tg = mm(mods, shard[...], NT)
    keep_ref[...] = tg[0:2]
    send_ref[...] = tg[2:4]


def ada_part(pos, pair, got, shard, parts, after):
    rows, width = shard.shape
    out = (UNIT, parts[0].shape[1] + width * rows // UNIT + SMALL)
    args = (pair, got, shard, *parts)
    return call(
        partial(ada_kernel, len(parts)), pos, args, [once(a.shape) for a in args],
        [sds(out, BF), sds((2, rows), F32), sds((2, rows), F32)], [once(out), once((2, rows)), once((2, rows))], (1,),
        [pltpu.VMEM((4, pair.shape[1]), F32)], "ada_part", after,
    )


def unpack_kernel(plan, pos, *refs):
    half = UNIT // 2
    count = len(plan)
    outs = refs[2 * count :]
    for i, moves in enumerate(plan):
        for which, ref in enumerate(refs[2 * i : 2 * i + 2]):
            for out, row, col, at, width in moves:
                place = pos[1] ^ which
                if row is None:
                    outs[out][:, pl.ds(pl.multiple_of(place * width, 128), width)] = ref[:, at : at + width].astype(F32)
                    continue
                base = pl.multiple_of(row + place * half, half)
                outs[out][pl.ds(base, half), col : col + width] = ref[:, at : at + width].astype(F32)


def unpack(pos, plan, pairs, shapes, after):
    args = [a for pair in pairs for a in pair]
    return call(
        partial(unpack_kernel, plan), pos, args, [once(a.shape) for a in args],
        [sds(s, F32) for s in shapes], [once(s) for s in shapes], (1,), [], "unpack", after,
    )


def mlp_rest_kernel(units, span, pos, near, far, down_in, up_in, down, up):
    half = UNIT // 2
    width = down.shape[1]
    block, owner = pl.program_id(0), pl.program_id(1)
    for which, ref in enumerate((near, far)):
        place = pos[1] ^ which

        @pl.when(owner == 0)
        def _():
            for k in range(TILE // UNIT):
                base = pl.multiple_of(k * UNIT + place * half, half)
                at = pl.multiple_of((block * (TILE // UNIT) + k) * width, 128)
                down[pl.ds(base, half), :] = ref[:, pl.ds(at, width)].astype(F32)

        for k in range(units):
            base = pl.multiple_of(k * UNIT + place * half, half)
            at = pl.multiple_of(span // UNIT * width + (owner * units + k) * span + block * TILE, 128)
            up[pl.ds(base, half), :] = ref[:, pl.ds(at, TILE)].astype(F32)


def mlp_rest(pos, pair, down, up, start, span, after):
    afters = after if isinstance(after, tuple) else (after,)
    hidden, width = down.shape
    units = up.shape[0] // UNIT
    per, base = hidden // TILE, start // TILE
    anywhere = pl.BlockSpec(memory_space=pl.ANY)
    args = (*pair, down, up)
    return call(
        partial(mlp_rest_kernel, units, span), pos, args, [once(a.shape) for a in pair] + [anywhere] * 2,
        [sds(down.shape, F32), sds(up.shape, F32)],
        [
            pl.BlockSpec((TILE, width), lambda j, i, *_: (base + j, 0)),
            pl.BlockSpec((up.shape[0], TILE), lambda j, i, *_: (0, i * per + base + j)),
        ],
        (span // TILE, 4), [], "mlp_rest", afters, aliases={1 + len(afters) + 2: 0, 1 + len(afters) + 3: 1},
    )


ORDER = ("g1", "F2", "MB", "g1", "g2", "Bb", "g1", "g2", "qb", "Ba", "g1", "g2", "qb", "qa", "IB", "g1", "qb", "g2", "row", "qa", "tg", "g1", "qb", "qa", "g2", "qb", "qa", "U1", "g2", "qb", "qa", "U2", "qb", "qa", "qa")
ROW_FIRST = {"g1": True, "g2": True, "qb": True}
WIDE_FIRST = True


def rotary_tables(length):
    half = HEAD_DIM // 2
    frequency = 10000.0 ** (-2.0 * np.arange(half) / HEAD_DIM)
    angles = np.arange(length)[:, None] * frequency[None, :]
    cos, sin = np.cos(angles), np.sin(angles)
    table = lambda *parts: jnp.asarray(np.concatenate(parts, axis=1).astype(np.float32))
    return table(cos, cos, cos, cos), table(-sin, sin, -sin, sin)


def local(
    mesh, block_input, cotangent, time_embed, ada_weight, ada_bias, attn_gain, qkv_weight, out_weight,
    mlp_gain, up_weight, up_bias, down_weight, down_bias,
):
    net = Net(mesh)
    length, width = block_input.shape
    f = net.f
    pos = jnp.stack([f] + [(net.d // bit) % 2 for bit in bits_of(net.dp)]).astype(jnp.int32)
    cond = time_embed.shape[1]
    quarter = width // 4
    ada_rows = ada_weight.shape[0]
    hidden_quarter = down_weight.shape[0]
    third = hidden_quarter // 3
    start_1, one = (0, 2 * third) if WIDE_FIRST else (2 * third, third)
    start_2, two = (2 * third, third) if WIDE_FIRST else (0, 2 * third)
    cols = HEADS_PER_STEP * HEAD_DIM
    groups = width // cols
    w = width
    cos, sin = rotary_tables(length)
    by_seq = lambda rel: jnp.take(rel, jnp.arange(4) ^ f, axis=0)

    units = quarter // UNIT
    in_groups = lambda a, b: [
        (0, k * UNIT, part * w + j * cols, cols) for k in range(units) for j in range(a, b) for part in range(3)
    ]
    of_up = lambda start, size: [
        (0, k * UNIT, i * hidden_quarter + start, size) for k in range(units) for i in range(4)
    ]
    of_down = lambda start, size: [(2, start + k * UNIT, 0, w) for k in range(size // UNIT)]
    rows = lambda v, at, n: lax.dynamic_slice_in_dim(v, at, n, 0)
    far_of = lambda near, far: (near, far, net.core_swap(near), net.core_swap(far))

    te_got = net.core_swap(time_embed)
    half_a, half_b = pack_halves(pos, [in_groups(0, 1), in_groups(1, groups)], [qkv_weight])
    half_a, attn_gain = tie(half_a, attn_gain)
    te = jnp.concatenate([time_embed, te_got], axis=0)
    te, half_b, attn_gain = tie(te, half_b, attn_gain)
    smalls = (attn_gain, mlp_gain, down_bias, up_bias, ada_bias)
    small = jnp.concatenate(smalls).reshape(1, -1)
    small_got = net.core_swap(small)
    te = jnp.concatenate([te, net.row_swap(te)], axis=0)
    near_a = net.row_swap(half_a)
    part = jnp.dot(
        lax.dynamic_slice_in_dim(by_seq(te), f * ada_rows, ada_rows, 1), ada_weight, preferred_element_type=F32
    )
    part_send = rows(part, 2 * (1 - net.row), 2)
    part_got = net.row_swap(part_send)
    small = jnp.concatenate([small, small_got], axis=0)
    small_far = net.row_swap(small)
    near_b = net.row_swap(half_b)
    partner_qkv = net.core_swap(qkv_weight)
    far_a = net.dp_swap(near_a, 1)
    up_weight, out_weight, down_weight, part_send = tie(up_weight, out_weight, down_weight, part_send)
    half_1, half_2, half_3 = pack_halves(
        pos,
        [
            of_up(start_1, one) + [(1, k * UNIT, 0, w) for k in range(units)], of_down(start_1, one),
            of_up(start_2, two) + of_down(start_2, two),
        ],
        [up_weight, out_weight, down_weight],
    )
    far_a = far_of(near_a, far_a)
    small = by_seq(jnp.concatenate([small, small_far], axis=0))
    part = rows(part, 2 * net.row, 2) + part_got
    cuts = np.cumsum([0] + [v.shape[0] for v in smalls])
    gain_a, gain_m, bias_d, bias_u, bias_ada = (
        small[:, cuts[i] : cuts[i + 1]].astype(F32).reshape(1, -1) for i in range(5)
    )
    mod = rows(part, net.core, 1) + net.core_swap(rows(part, 1 - net.core, 1)) + bias_ada
    near_b, block_input = tie(near_b, block_input)
    far_b = net.dp_swap(near_b, 1)
    near_1, near_2, near_3 = (net.row_swap(v) for v in (half_1, half_2, half_3))
    partner_out, partner_up, partner_down = (net.core_swap(v) for v in (out_weight, up_weight, down_weight))

    attn_in, *saved_a = attention_forward(
        pos, 0, 1, True, block_input, gain_a, mod, (qkv_weight, partner_qkv, *far_a), cos, sin
    )
    far_b, near_1, attn_in = tie(far_b, near_1, attn_in)
    far_b = far_of(near_b, far_b)
    far_1 = net.dp_swap(near_1, 1)
    saved_b = attention_forward(
        pos, 1, groups - 1, False, attn_in, gain_a, mod, (qkv_weight, partner_qkv, *far_b), cos, sin
    )
    if WIDE_FIRST:
        far_1, near_2, o_b = tie(far_1, near_2, saved_b[4])
    else:
        far_1, near_2, near_3, o_b = tie(far_1, near_2, near_3, saved_b[4])
    far_1 = far_of(near_1, far_1)
    far_2 = net.dp_swap(near_2, 1)
    os = (saved_a[4], o_b)
    branch, middle, mlp_in, mlp_grad, out_full = middle_forward(
        pos, os, block_input, cotangent, mod, gain_m, out_weight, partner_out, far_1, units * 4 * one
    )
    far_2, near_3, mlp_in = tie(far_2, near_3, mlp_in)
    far_2 = far_of(near_2, far_2)
    far_3 = net.dp_swap(near_3, 1)
    mb, back, bias_g1, *s1 = mlp(
        pos, mlp_in, mlp_grad, bias_u, (up_weight, partner_up, *far_1), (down_weight, partner_down, *far_2), 0,
        start_1, one, None, True,
    )
    far_3, mb, *s1 = tie(far_3, mb, *s1)
    far_3 = far_of(near_3, far_3)
    chunks = {"g1": Chunk(net, s1, ROW_FIRST["g1"])}
    state = {}

    def run(name, after):
        if name == "F2":
            mb2, back2, state["bias_g2"], *s2 = mlp(
                pos, mlp_in, mlp_grad, bias_u, (up_weight, partner_up, *far_3), (down_weight, partner_down, *far_3),
                units * 4 * two, start_2, two, (mb, back), True, after,
            )
            chunks["g2"] = Chunk(net, s2, ROW_FIRST["g2"])
            state["mb"], state["back"] = mb2, back2
            return back2
        if name == "MB":
            state["mid"], state["out"], state["low"], state["do"], state["sums_m"] = middle_back(
                pos, state["back"], state["mb"], middle, branch, cotangent, mod, gain_m, bias_d, out_full, after
            )
            return state["do"]
        if name == "Bb":
            state["grad_b"], *sb = attention_back(
                pos, saved_b, state["do"], cols, attn_in, cos, sin, (os, state["low"]), after
            )
            chunks["qb"] = Chunk(net, sb, ROW_FIRST["qb"])
            return state["grad_b"]
        if name == "Ba":
            state["grad_a"], *sa = attention_back(pos, saved_a, state["do"], 0, attn_in, cos, sin, None, after)
            chunks["qa"] = Chunk(net, sa, True, extend)
            return state["grad_a"]
        if name == "IB":
            state["input_grad"], row = input_back(
                pos, (state["grad_a"], state["grad_b"]), (0, 1), (qkv_weight, partner_qkv, *far_a, *far_b),
                block_input, state["mid"], mod, gain_a, state["sums_m"], time_embed, (bias_g1, state["bias_g2"]) if WIDE_FIRST else (state["bias_g2"], bias_g1), after,
            )
            state["row"], state["row_got"] = row, net.core_swap(row)
            return state["input_grad"]
        if name == "row":
            state["pair"] = jnp.concatenate([*follow(after, state["row"]), state["row_got"]], axis=0)
            state["pair_got"] = net.row_swap(state["pair"])
            return state["pair"]
        if name == "tg":
            keep, = follow(after, state["tg_keep"])
            state["give"] = jnp.concatenate([keep[1:2], state["tg_got"][1:2]], axis=0)
            state["given"] = net.core_swap(state["give"])
            return state["give"]
        if name == "U1":
            plan = [(0, start_1 + k * UNIT, 0, k * w, w) for k in range(one // UNIT)] + [
                (1, k * UNIT, i * hidden_quarter + start_1, one // UNIT * w + (i * units + k) * one, one)
                for i in range(4) for k in range(units)
            ]
            state["down_grad"], state["up_grad"] = unpack(
                pos, [plan], [chunks["g1"].ready], ((hidden_quarter, w), (quarter, 4 * hidden_quarter)), after
            )
            return state["up_grad"]
        if name == "U2":
            state["down_grad"], state["up_grad"] = mlp_rest(
                pos, chunks["g2"].ready, state["down_grad"], state["up_grad"], start_2, two, after
            )
            return state["up_grad"]
        return chunks[name].step(after)

    def extend(parts, after):
        merged, state["tg_keep"], state["tg_send"] = ada_part(
            pos, state["pair"], state["pair_got"], ada_weight, [p.base for p in parts], after
        )
        state["tg_got"] = net.row_swap(state["tg_send"])
        return merged

    def finish(names, after):
        while any(chunks[n].where != "end" for n in names):
            for n in names:
                if chunks[n].where != "end":
                    after = run(n, after)
        return after

    after = None
    for name in ORDER:
        if name in chunks and chunks[name].where == "end":
            continue
        if name in ("U1", "U2"):
            after = finish(["g" + name[1]], after)
        after = run(name, after)
    after = finish(["qa", "qb"], after)

    block_output, input_grad = state["out"], state["input_grad"]
    down_grad, up_grad = state["down_grad"], state["up_grad"]
    wide = units * 3 * cols
    of = lambda j, at: [
        (0, k * UNIT, part_ * w + j * cols, at + k * 3 * cols + part_ * cols, cols)
        for k in range(units) for part_ in range(3)
    ]
    ada_part_width = 6 * w * ada_rows // UNIT
    qa, qb = chunks["qa"].ready, chunks["qb"].ready
    ada_weight_grad, small_sums = unpack(
        pos, [[(0, None, 0, wide, ada_part_width), (1, 0, 0, wide + ada_part_width, SMALL)]], [qa],
        (ada_weight.shape, (UNIT, SMALL)), after,
    )
    total = small_sums.reshape(-1)
    own_cols = lambda start, size: lax.dynamic_slice_in_dim(total, start + f * size, size, 0)
    ada_bias_grad = own_cols(0, 6 * w // 4)
    attn_gain_grad = own_cols(6 * w, quarter)
    mlp_gain_grad = own_cols(7 * w, quarter)
    down_bias_grad = own_cols(8 * w, quarter)
    up_bias_grad = own_cols(9 * w, up_bias.shape[0])
    tg_keep, tg_got, given = state["tg_keep"], state["tg_got"], state["given"]
    parts = jnp.concatenate([tg_keep[0:1], given[0:1], tg_got[0:1], given[1:2]], axis=0)
    time_grad = by_seq(parts).reshape(1, cond)
    plan = [
        [m for j in range(1, groups) for m in of(j, (j - 1) * wide)]
        + [(1, k * UNIT, 0, (groups - 1) * wide + k * w, w) for k in range(units)],
        of(0, 0),
    ]
    qkv_grad, out_grad = unpack(
        pos, plan, (qb, qa), ((quarter, 3 * w), (quarter, w)),
        (ada_bias_grad, attn_gain_grad, mlp_gain_grad, down_bias_grad, up_bias_grad, time_grad),
    )
    return (
        block_output, input_grad, time_grad, ada_weight_grad, ada_bias_grad, attn_gain_grad, qkv_grad, out_grad,
        mlp_gain_grad, up_grad, up_bias_grad, down_grad, down_bias_grad,
    )


def solution(mesh):
    rows, shard, line = P(("dp", "fsdp"), None), P("fsdp", None), P("fsdp")
    return jax.shard_map(
        partial(local, mesh),
        mesh=mesh,
        in_specs=(rows, rows, rows, shard, line, line, shard, shard, line, shard, line, shard, line),
        out_specs=(rows, rows, rows, shard, line, line, shard, shard, line, shard, line, shard, line),
        check_vma=False,
    )
```

```python
from functools import partial

import numpy as np

import jax
import jax.numpy as jnp
from jax import lax
from jax.experimental import pallas as pl
from jax.experimental.pallas import tpu as pltpu
from jax.sharding import PartitionSpec as P

HEAD_DIM = 64
BF = jnp.bfloat16
F32 = jnp.float32
NN = (((1,), (0,)), ((), ()))
NT = (((1,), (1,)), ((), ()))
TN = (((0,), (0,)), ((), ()))
VMEM_LIMIT = 60 * 2**20
HEADS_PER_STEP = 4
GELU_C = 0.7978845608028654
GELU_A = 0.044715


def mm(a, b, dims=NN):
    return lax.dot_general(a, b, dims, preferred_element_type=F32)


UNIT = 64


def swap(value, axis, size, bit):
    return lax.ppermute(value, axis, [(i, i ^ bit) for i in range(size)])


def bits_of(size):
    bits, bit = [], 1
    while bit < size:
        bits.append(bit)
        bit *= 2
    return bits


def tie(*values):
    return lax.optimization_barrier(values)


class Net:
    def __init__(self, mesh):
        self.dp = mesh.shape["dp"]
        self.fsdp = mesh.shape["fsdp"]
        self.d = lax.axis_index("dp")
        self.f = lax.axis_index("fsdp")
        self.core = self.f % 2
        self.row = self.f // 2
        self.side = self.d % 2
        self.zero = self.d // self.dp

    def core_swap(self, v):
        return swap(v, "fsdp", self.fsdp, 1)

    def row_swap(self, v):
        return swap(v, "fsdp", self.fsdp, 2)

    def dp_swap(self, v, bit):
        return swap(v, "dp", self.dp, bit)


def follow(after, *values):
    if after is None:
        return list(values)
    return list(tie(after, *values)[1:])


class Part:
    def __init__(self, base, cuts=()):
        self.base, self.cuts = base, cuts

    def cut(self, which):
        return Part(self.base, self.cuts + (which,))

    def read(self):
        v = self.base
        for which in self.cuts:
            half = v.shape[0] // 2
            v = lax.dynamic_slice_in_dim(v, which * half, half, 0)
        return v.astype(F32)


def add(parts):
    return sum(p.read() for p in parts).astype(BF)


def hold(after, parts):
    bases = []
    for p in parts:
        if not any(p.base is b for b in bases):
            bases.append(p.base)
    held = follow(after, *bases)
    return [Part(next(h for h, b in zip(held, bases) if b is p.base), p.cuts) for p in parts]


def chunk_steps(net, keep, send, row_first, extend):
    got, after = yield ("core", send)
    kept = Part(*follow(after, keep))
    came = Part(got)
    near, far = [kept.cut(net.zero), came.cut(net.zero)], [kept.cut(1 + net.zero), came.cut(1 + net.zero)]
    bits = bits_of(net.dp)
    todo = (["row"] + bits[:-1]) if row_first else (bits[:1] + ["row"] + bits[1:-1])
    split = True
    for where in todo:
        if where == "row":
            got, after = yield (where, add(far))
            near = hold(after, near) + [Part(got)]
            split = False
            if extend:
                near = [Part(extend(near, after))]
            continue
        which = (net.d // where) % 2
        give = lambda parts: add([p.cut(1 - which) for p in parts])
        stay = lambda parts: [p.cut(which) for p in parts]
        if split:
            (near_got, far_got), after = yield (where, tie(give(near), give(far)))
            both = hold(after, near + far)
            near, far = stay(both[: len(near)]) + [Part(near_got)], stay(both[len(near) :]) + [Part(far_got)]
        else:
            got, after = yield (where, give(near))
            near = stay(hold(after, near)) + [Part(got)]
    own = add(near)
    got, after = yield (bits[-1], own)
    total = add(hold(after, [Part(own)]) + [Part(got)])
    for bit in reversed(bits[:-1]):
        got, after = yield (bit, total)
        if bit != 1:
            first = (net.d // bit) % 2 == 0
            (total,) = follow(after, total)
            total = jnp.concatenate([jnp.where(first, total, got), jnp.where(first, got, total)], axis=0)
    yield ("end", (total, got))


class Chunk:
    def __init__(self, net, shares, row_first=True, extend=None):
        self.net = net
        self.steps = chunk_steps(net, *shares, row_first, extend)
        self.where, self.ready = next(self.steps)
        self.got = net.core_swap(self.ready)

    def step(self, after):
        self.where, self.ready = self.steps.send((self.got, after))
        if self.where == "end":
            return after
        if self.where == "row":
            self.got = self.net.row_swap(self.ready)
        elif isinstance(self.ready, (list, tuple)):
            self.got = [self.net.dp_swap(v, self.where) for v in self.ready]
            return self.ready[0]
        else:
            self.got = self.net.dp_swap(self.ready, self.where)
        return self.ready


def normed(values):
    centre = jnp.mean(values, axis=-1, keepdims=True)
    centred = values - centre
    spread = jnp.mean(centred * centred, axis=-1, keepdims=True)
    r = lax.rsqrt(spread + 1e-05)
    return centred * r, r


def norm_back(grad, n, r, gain, scale):
    e = grad * (1.0 + scale) * gain
    return r * (e - jnp.mean(e, -1, keepdims=True) - n * jnp.mean(e * n, -1, keepdims=True))


def column_sum(v):
    return jnp.sum(v, axis=0, keepdims=True)


def of_head(shape, head):
    return (lax.broadcasted_iota(jnp.int32, shape, 1) // HEAD_DIM) == head


def turn(v, cos, sin):
    half = HEAD_DIM // 2
    low = (lax.broadcasted_iota(jnp.int32, v.shape, 1) // half) % 2 == 0
    width = v.shape[1]
    other = jnp.where(low, pltpu.roll(v, width - half, 1), pltpu.roll(v, half, 1))
    return v * cos + other * sin


def place_near(full, pos, own, partner, cols=((0, 0, None),)):
    rows = own.shape[0]
    for ref, flip in ((own, 0), (partner, 1)):
        base = pl.multiple_of((pos[0] ^ flip) * rows, UNIT)
        for to, at, width in cols:
            width = width or full.shape[1]
            full[pl.ds(base, rows), to : to + width] = ref[:, at : at + width]


def place_far(full, pos, far, rows, at, width):
    half = UNIT // 2
    for i, ref in enumerate(far):
        for k in range(rows // UNIT):
            base = pl.multiple_of((pos[0] ^ (2 + i // 2)) * rows + k * UNIT + (pos[1] ^ (i % 2)) * half, half)
            full[pl.ds(base, half), :] = ref[:, at + k * width : at + (k + 1) * width]


def store_shares(pos, grad, shares, at):
    quarter, width = grad.shape[0] // 4, grad.shape[1]
    for owner in range(4):
        rel = pos[0] ^ owner
        blocks = [
            grad[owner * quarter + k * UNIT : owner * quarter + (k + 1) * UNIT].astype(BF)
            for k in range(quarter // UNIT)
        ]
        put_shares(rel, blocks, shares, at)


def put_shares(rel, blocks, shares, at):
    row = pl.multiple_of(rel // 2 * UNIT, UNIT)

    def put(ref):
        for k, block in enumerate(blocks):
            ref[pl.ds(row, UNIT), at(k, block.shape[1])] = block

    for index in range(2):
        pl.when(rel % 2 == index)(partial(put, shares[index]))


def pack_kernel(plan, pos, *refs):
    half = UNIT // 2
    outs = refs[len(refs) - len(plan) :]
    for out, moves in zip(outs, plan):
        to = 0
        for src, row, col, width in moves:
            base = pl.multiple_of(row + pos[1] * half, half)
            out[:, to : to + width] = refs[src][pl.ds(base, half), col : col + width]
            to += width


def pack_halves(pos, plan, arrays):
    outs = [sds((UNIT // 2, sum(m[3] for m in moves)), BF) for moves in plan]
    return call(
        partial(pack_kernel, plan), pos, arrays, [once(a.shape) for a in arrays], outs, [once(o.shape) for o in outs],
        (1,), [], "pack_halves", cost=10,
    )


def attention_kernel(group, first, pos, x_ref, gain_ref, mod_ref, own, partner, n0, n1, n2, n3, cos_ref, sin_ref, *rest):
    if first:
        in_ref, q_ref, k_ref, v_ref, p_ref, o_ref, full = rest
    else:
        q_ref, k_ref, v_ref, p_ref, o_ref, full = rest
        in_ref = x_ref
    cols = q_ref.shape[1]
    step = pl.program_id(0)
    width = x_ref.shape[1]

    @pl.when(step == 0)
    def _():
        place_groups(full, pos, own, partner, (n0, n1, n2, n3), group, cols)
        if first:
            n, _ = normed(x_ref[...].astype(F32))
            shift, scale = mod_ref[:, :width], mod_ref[:, width : 2 * width]
            in_ref[...] = (n * gain_ref[...] * (1.0 + scale) + shift).astype(BF)

    base = pl.multiple_of(step * 3 * cols, cols)
    attn_in = in_ref[...]
    cos, sin = cos_ref[...], sin_ref[...]
    q_all = mm(attn_in, full[:, pl.ds(base, cols)])
    k_all = mm(attn_in, full[:, pl.ds(base + cols, cols)])
    v_ref[...] = mm(attn_in, full[:, pl.ds(base + 2 * cols, cols)]).astype(BF)
    for pair in range(cols // 128):
        sl = slice(pair * 128, pair * 128 + 128)
        q = turn(q_all[:, sl], cos, sin).astype(BF) * BF(HEAD_DIM**-0.5)
        k = turn(k_all[:, sl], cos, sin).astype(BF)
        q_ref[:, sl] = q
        k_ref[:, sl] = k
        v = v_ref[:, sl]
        outs = []
        for h in range(2):
            kh = jnp.where(of_head(k.shape, h), k, jnp.zeros_like(k))
            s = mm(kh, q, NT)
            e = jnp.exp(s - jnp.max(s, axis=0, keepdims=True))
            p = (e * (1.0 / jnp.sum(e, axis=0, keepdims=True))).astype(BF)
            p_ref[2 * pair + h] = p
            outs.append(mm(p, v, TN))
        o_ref[:, sl] = jnp.where(of_head(outs[0].shape, 0), outs[0], outs[1]).astype(BF)


def whole(shape):
    return pl.BlockSpec(shape, lambda *_: (0,) * len(shape))


def once(shape):
    return pl.BlockSpec(shape, lambda *_: (0,) * len(shape), pipeline_mode=pl.Buffered(1))


def place_groups(full, pos, own, partner, far, group, cols):
    width = own.shape[1] // 3
    moves = [
        ((3 * j + part) * cols, part * width + (group + j) * cols, cols)
        for j in range(full.shape[1] // (3 * cols)) for part in range(3)
    ]
    place_near(full, pos, own, partner, moves)
    place_far(full, pos, far, own.shape[0], 0, full.shape[1])


def sds(shape, dtype):
    return jax.ShapeDtypeStruct(shape, dtype)


def call(body, pos, args, in_specs, outs, out_specs, grid, scratch, name, after=None, cost=0, aliases={}):
    if after is not None:
        inner, afters = body, after if isinstance(after, tuple) else (after,)
        body = lambda pos_ref, *refs: inner(pos_ref, *refs[len(afters) :])
        args, in_specs = (*afters, *args), [pl.BlockSpec(memory_space=pl.ANY)] * len(afters) + [*in_specs]
    return pl.pallas_call(
        body,
        grid_spec=pltpu.PrefetchScalarGridSpec(
            num_scalar_prefetch=1, grid=grid, in_specs=in_specs, out_specs=out_specs, scratch_shapes=scratch
        ),
        out_shape=outs,
        compiler_params=pltpu.CompilerParams(vmem_limit_bytes=VMEM_LIMIT),
        cost_estimate=pl.CostEstimate(flops=1024 + cost * 10**9, bytes_accessed=1024, transcendentals=0),
        input_output_aliases=aliases,
        name=name,
    )(pos, *args)


def attention_forward(pos, group, count, first, x, gain, mod, pieces, cos, sin):
    length, width = x.shape
    cols = HEADS_PER_STEP * HEAD_DIM
    row = pl.BlockSpec((length, cols), lambda j, *_: (0, j))
    args = (x, gain, mod, *pieces, cos, sin)
    qkv_out = sds((length, count * cols), BF)
    outs = [qkv_out] * 3 + [sds((count * HEADS_PER_STEP, length, length), BF), qkv_out]
    specs = [row, row, row, pl.BlockSpec((HEADS_PER_STEP, length, length), lambda j, *_: (j, 0, 0)), row]
    if first:
        outs, specs = [sds(x.shape, BF)] + outs, [whole(x.shape)] + specs
    return call(
        partial(attention_kernel, group, first), pos, args, [once(a.shape) for a in args], outs, specs,
        (count,), [pltpu.VMEM((width, count * 3 * cols), BF)], "attention_forward", cost=30,
    )


ROWS = 192


def rows_of(shape):
    return pl.BlockSpec((ROWS, shape[1]), lambda i, *_: (i, 0))


def middle_kernel(count, units, pos, *refs):
    o_refs, refs = refs[:count], refs[count:]
    x_ref, g_ref, mod_ref, gain_ref, own, partner, *far = refs[: 6 + 4 * units]
    branch_ref, middle_ref, in_ref, grad_ref, full = refs[6 + 4 * units :]
    width = x_ref.shape[1]
    half = UNIT // 2

    @pl.when(pl.program_id(0) == 0)
    def _():
        place_near(full, pos, own, partner)
        for i in range(4):
            for k in range(units):
                base = (pos[0] ^ (2 + i // 2)) * own.shape[0] + k * UNIT + (pos[1] ^ (i % 2)) * half
                full[pl.ds(pl.multiple_of(base, half), half), :] = far[i * units + k][...]

    piece = lambda i: mod_ref[:, i * width : (i + 1) * width]
    branch, at = jnp.zeros(x_ref.shape, F32), 0
    for o_ref in o_refs:
        branch += mm(o_ref[...], full[at : at + o_ref.shape[1], :])
        at += o_ref.shape[1]
    branch_ref[...] = branch
    middle = x_ref[...].astype(F32) + piece(2) * branch
    middle_ref[...] = middle
    n, _ = normed(middle)
    in_ref[...] = (n * gain_ref[...] * (1.0 + piece(4)) + piece(3)).astype(BF)
    grad_ref[...] = (piece(5) * g_ref[...].astype(F32)).astype(BF)


def middle_forward(pos, os, x, g, mod, gain, own, partner, far, at):
    length, width = x.shape
    units = own.shape[0] // UNIT
    args = (*os, x, g, mod, gain, own, partner, *[p for p in far for _ in range(units)])
    specs = [rows_of(a.shape) for a in (*os, x, g)] + [once(a.shape) for a in (mod, gain, own, partner)]
    specs += [
        pl.BlockSpec((UNIT // 2, width), lambda *_, k=k: (0, at // width + k), pipeline_mode=pl.Buffered(1))
        for _ in far for k in range(units)
    ]
    full = sds((width, width), BF)
    return call(
        partial(middle_kernel, len(os), units), pos, args, specs,
        [sds(x.shape, F32), sds(x.shape, F32), sds(x.shape, BF), sds(x.shape, BF), full],
        [rows_of(x.shape)] * 4 + [whole(full.shape)], (length // ROWS,), [], "middle_forward", cost=30,
    )


TILE = 256


def mlp_kernel(start, span, first, joint, down_at, pos, *refs):
    tiles = span // TILE
    refs = list(refs)
    take = lambda n: [refs.pop(0) for _ in range(n)]
    in_ref, grad_ref, bias_ref = take(3)
    own_up, partner_up = take(tiles), take(tiles)
    units = own_up[0].shape[0] // UNIT
    far_up = [take(units) for _ in range(4)]
    own_down, partner_down, *far_down = take(6)
    if not first:
        branch_in, back_in = take(2)
    branch_ref, back_ref, bias_grad_ref = take(3)
    shares_d = take(2)
    shares_u = shares_d if joint else take(2)
    up, down = refs
    step = pl.program_id(0)
    hidden = 4 * own_down.shape[0]
    rows = own_up[0].shape[0]
    half = UNIT // 2
    f, side = pos[0], pos[1]

    @pl.when(step == 0)
    def _():
        if first:
            branch_ref[...] = jnp.zeros_like(branch_ref)
            back_ref[...] = jnp.zeros_like(back_ref)
        else:
            branch_ref[...] = branch_in[...]
            back_ref[...] = back_in[...]

    for many, flip in ((own_up, 0), (partner_up, 1)):
        base = pl.multiple_of((f ^ flip) * rows, UNIT)
        for i, ref in enumerate(many):
            up[pl.ds(base, rows), i * TILE : (i + 1) * TILE] = ref[...]
    for i, many in enumerate(far_up):
        for k, ref in enumerate(many):
            base = pl.multiple_of((f ^ (2 + i // 2)) * rows + k * UNIT + (side ^ (i % 2)) * half, half)
            up[pl.ds(base, half), :] = ref[...]

    rel = f ^ step
    width = in_ref.shape[1]
    for index, ref in ((0, own_down), (1, partner_down)):

        @pl.when(rel == index)
        def _():
            down[...] = ref[start : start + span, :]

    for index, pair in ((2, far_down[:2]), (3, far_down[2:])):

        @pl.when(rel == index)
        def _():
            for h, ref in enumerate(pair):
                for k in range(span // UNIT):
                    base = pl.multiple_of(k * UNIT + (side ^ h) * half, half)
                    down[pl.ds(base, half), :] = ref[:, down_at + k * width : down_at + (k + 1) * width]

    mlp_in, mlp_grad = in_ref[...], grad_ref[...]
    up_t, down_t = up[...], down[...]
    base = pl.multiple_of(step * (hidden // 4) + start, 128)
    pre = mm(mlp_in, up_t) + bias_ref[:, pl.ds(base, span)]
    t = jnp.tanh(GELU_C * (pre + GELU_A * (pre * pre * pre)))
    activ = (0.5 * pre * (1.0 + t)).astype(BF)
    slope = 0.5 * (1.0 + t) + (0.5 * GELU_C) * pre * (1.0 - t * t) * (1.0 + (3.0 * GELU_A) * (pre * pre))
    pre_grad = (mm(mlp_grad, down_t, NT) * slope).astype(BF)
    bias_grad_ref[:, pl.ds(pl.multiple_of(step * span, span), span)] = column_sum(pre_grad.astype(F32))
    branch_ref[...] += mm(activ, down_t)
    back_ref[...] += mm(pre_grad, up_t, NT)
    dd = mm(activ, mlp_grad, TN).astype(BF)
    put_shares(rel, [dd[k * UNIT : (k + 1) * UNIT] for k in range(span // UNIT)], shares_d, lambda k, w: slice(k * w, (k + 1) * w))
    after = (span // UNIT) * width if joint else 0
    at = lambda k, w: pl.ds(pl.multiple_of(after + (step * units + k) * w, 128), w)
    store_shares(pos, mm(mlp_in, pre_grad, TN), shares_u, at)


def mlp(pos, mlp_in, mlp_grad, bias, ups, downs, down_at, start, span, carried, joint, after=None):
    length, width = mlp_in.shape
    first = carried is None
    rows, hidden = ups[0].shape
    tiles, units, per = span // TILE, rows // UNIT, hidden // 4 // TILE
    args = [mlp_in, mlp_grad, bias]
    specs = [once(a.shape) for a in args]
    for ref in ups[:2]:
        for i in range(tiles):
            args.append(ref)
            specs.append(pl.BlockSpec((rows, TILE), lambda s, *_, i=i: (0, s * per + start // TILE + i)))
    for ref in ups[2:]:
        for k in range(units):
            args.append(ref)
            specs.append(pl.BlockSpec((UNIT // 2, span), lambda s, *_, k=k: (0, k * 4 + s)))
    args += list(downs)
    specs += [once(a.shape) for a in downs]
    if not first:
        args += list(carried)
        specs += [once(a.shape) for a in carried]
    acc = sds((length, width), F32)
    cols_d, cols_u = (span // UNIT) * width, 4 * units * span
    shares = [sds((2 * UNIT, c), BF) for c in ((cols_d + cols_u,) if joint else (cols_d, cols_u)) for _ in range(2)]
    return call(
        partial(mlp_kernel, start, span, first, joint, down_at), pos, args, specs,
        [acc, acc, sds((1, 4 * span), F32), *shares],
        [once((length, width))] * 2 + [once((1, 4 * span))] + [once(v.shape) for v in shares],
        (4,), [pltpu.VMEM((width, span), BF), pltpu.VMEM((span, width), BF)], "mlp_first" if first else "mlp_second", after,
        60 if first else 0,
    )


def add_sums(ref, sums):
    @pl.when(pl.program_id(0) == 0)
    def _():
        ref[...] = jnp.zeros_like(ref)

    for i, v in enumerate(sums):
        width = v.shape[1]
        ref[:, i * width : (i + 1) * width] += v


def middle_back_kernel(
    pos, back_ref, mlp_ref, middle_ref, branch_ref, g_ref, mod_ref, gain_ref, bias_ref, out_w,
    grad_ref, out_ref, low_ref, do_ref, sums_ref,
):
    width = g_ref.shape[1]
    piece = lambda i: mod_ref[:, i * width : (i + 1) * width]
    g = g_ref[...].astype(F32)
    middle = middle_ref[...]
    branch = branch_ref[...]
    gain = gain_ref[...]
    mlp_branch = mlp_ref[...] + bias_ref[...]
    out_ref[...] = (middle + piece(5) * mlp_branch).astype(BF)
    n, r = normed(middle)
    back = back_ref[...]
    back_sum = column_sum(back * n)
    grad = g + norm_back(back, n, r, gain, piece(4))
    grad_ref[...] = grad
    low = (piece(2) * grad).astype(BF)
    low_ref[...] = low
    sums = (
        column_sum(grad * branch),
        column_sum(back),
        back_sum * gain,
        column_sum(g * mlp_branch),
        back_sum * (1.0 + piece(4)),
        column_sum((piece(5) * g).astype(BF).astype(F32)),
    )
    add_sums(sums_ref, sums)
    do_ref[...] = mm(low, out_w[...], NT).astype(BF)


def middle_back(pos, back, mlp_branch, middle, branch, g, mod, gain, bias, out_w, after):
    length, width = g.shape
    args = (back, mlp_branch, middle, branch, g, mod, gain, bias, out_w)
    return call(
        middle_back_kernel, pos, args, [rows_of(a.shape) for a in args[:5]] + [once(a.shape) for a in args[5:]],
        [sds(g.shape, F32), sds(g.shape, BF), sds(g.shape, BF), sds(g.shape, BF), sds((1, 6 * width), F32)],
        [rows_of(g.shape)] * 4 + [whole((1, 6 * width))], (length // ROWS,), [], "middle_back", after, 60,
    )


def attention_back_kernel(extra, groups, pos, q_ref, k_ref, v_ref, p_ref, o_ref, do_ref, in_ref, cos_ref, sin_ref, *rest):
    rest = list(rest)
    if extra:
        o_all = [rest.pop(0) for _ in range(extra)]
        low_ref = rest.pop(0)
    grad_ref, *shares = rest
    cols = q_ref.shape[1]
    at = lambda k, w: slice(k * w, (k + 1) * w)

    def heads():
        cos, sin = cos_ref[...], -sin_ref[...]
        for pair in range(cols // 128):
            sl = slice(pair * 128, pair * 128 + 128)
            q, k, v, do = q_ref[:, sl], k_ref[:, sl], v_ref[:, sl], do_ref[:, sl]
            od = o_ref[:, sl].astype(F32) * do.astype(F32)
            dq, dk, dv = [], [], []
            for h in range(2):
                mask = of_head(v.shape, h)
                p = p_ref[2 * pair + h]
                dp = mm(jnp.where(mask, v, jnp.zeros_like(v)), do, NT)
                delta = jnp.sum(jnp.where(mask, od, 0.0).T, axis=0, keepdims=True)
                ds = (p.astype(F32) * (dp - delta)).astype(BF)
                dv.append(mm(p, do))
                dk.append(mm(ds, q))
                dq.append(mm(ds, k, TN))
            mask = of_head(q.shape, 0)
            both = lambda pair_: jnp.where(mask, pair_[0], pair_[1])
            grad_ref[:, sl] = turn(both(dq) * HEAD_DIM**-0.5, cos, sin).astype(BF)
            grad_ref[:, cols + pair * 128 : cols + pair * 128 + 128] = turn(both(dk), cos, sin).astype(BF)
            grad_ref[:, 2 * cols + pair * 128 : 2 * cols + pair * 128 + 128] = both(dv).astype(BF)
        store_shares(pos, mm(in_ref[...], grad_ref[...], TN), shares, at)

    if not extra:
        heads()
        return
    step = pl.program_id(0)
    pl.when(step < groups)(heads)

    @pl.when(step == groups)
    def _():
        low = low_ref[...]
        parts = [mm(o_[...], low, TN) for o_ in o_all]
        store_shares(pos, jnp.concatenate(parts, axis=0), shares, at)


def attention_back(pos, saved, do, do_at, attn_in, cos, sin, extra, after):
    q, k, v, p, o = saved
    length, width = attn_in.shape
    cols = HEADS_PER_STEP * HEAD_DIM
    groups = q.shape[1] // cols
    last = groups - 1
    row = pl.BlockSpec((length, cols), lambda j, *_: (0, jnp.minimum(j, last)))
    do_row = pl.BlockSpec((length, cols), lambda j, *_: (0, do_at // cols + jnp.minimum(j, last)))
    steps = groups + (1 if extra else 0)
    share = sds((2 * UNIT, steps * width // 4 // UNIT * 3 * cols), BF)
    share_spec = pl.BlockSpec((2 * UNIT, width // 4 // UNIT * 3 * cols), lambda j, *_: (0, j))
    args = [q, k, v, p, o, do, attn_in, cos, sin]
    specs = [row, row, row, pl.BlockSpec((HEADS_PER_STEP, length, length), lambda j, *_: (jnp.minimum(j, last), 0, 0)),
             row, do_row, once(attn_in.shape), once(cos.shape), once(sin.shape)]
    if extra:
        args += [*extra[0], extra[1]]
        specs += [once(a.shape) for a in (*extra[0], extra[1])]
    return call(
        partial(attention_back_kernel, len(extra[0]) if extra else 0, groups), pos, args, specs,
        [sds((length, 3 * groups * cols), BF)] + [share] * 2,
        [pl.BlockSpec((length, 3 * cols), lambda j, *_: (0, jnp.minimum(j, last)))] + [share_spec] * 2,
        (steps,), [], "attention_back", after,
    )


def input_back_kernel(starts, count, pos, *refs):
    grads, refs = refs[: len(starts)], refs[len(starts) :]
    own, partner, *far = refs[: 2 + 4 * len(starts)]
    x_ref, mid_ref, mod_ref, gain_ref, sums_m, te, *rest = refs[2 + 4 * len(starts) :]
    biases, (out_ref, row_ref, sums_ref, *fulls) = rest[:count], rest[count:]
    width = x_ref.shape[1]
    cols = HEADS_PER_STEP * HEAD_DIM

    @pl.when(pl.program_id(0) == 0)
    def _():
        for i, full in enumerate(fulls):
            place_groups(full, pos, own, partner, far[4 * i : 4 * i + 4], starts[i], cols)

    back = jnp.zeros(x_ref.shape, F32)
    for grad, full in zip(grads, fulls):
        back += mm(grad[...], full[...], NT)
    scale = mod_ref[:, width : 2 * width]
    gain = gain_ref[...]
    n, r = normed(x_ref[...].astype(F32))
    back_sum = column_sum(back * n)
    out_ref[...] = mid_ref[...] + norm_back(back, n, r, gain, scale)
    add_sums(sums_ref, (column_sum(back), back_sum * gain, back_sum * (1.0 + scale)))

    @pl.when(pl.program_id(0) == pl.num_programs(0) - 1)
    def _():
        w = width
        row_ref[:, : 2 * w] = sums_ref[:, : 2 * w].astype(BF)
        row_ref[:, 2 * w : 6 * w] = sums_m[:, : 4 * w].astype(BF)
        row_ref[:, 6 * w : 7 * w] = sums_ref[:, 2 * w :].astype(BF)
        row_ref[:, 7 * w : 9 * w] = sums_m[:, 4 * w :].astype(BF)
        at = 9 * w
        spans = [b.shape[1] // 4 for b in biases]
        for i in range(4):
            for b, span in zip(biases, spans):
                row_ref[:, at : at + span] = b[:, i * span : (i + 1) * span].astype(BF)
                at += span
        row_ref[:, at:] = te[...]


def input_back(pos, grads, starts, weights, x, mid, mod, gain, sums_m, te, biases, after):
    length, width = x.shape
    args = (*grads, *weights, x, mid, mod, gain, sums_m, te, *biases)
    split = {*range(len(grads))} | {len(grads) + len(weights), len(grads) + len(weights) + 1}
    specs = [rows_of(a.shape) if i in split else once(a.shape) for i, a in enumerate(args)]
    row = (1, 9 * width + sum(b.shape[1] for b in biases) + te.shape[1])
    return call(
        partial(input_back_kernel, starts, len(biases)), pos, args, specs,
        [sds(x.shape, F32), sds(row, BF)], [rows_of(x.shape), whole(row)], (length // ROWS,),
        [pltpu.VMEM((1, 3 * width), F32)] + [pltpu.VMEM((width, g.shape[1]), BF) for g in grads], "input_back", after,
    )


SMALL = 256


def ada_kernel(count, pos, pair, got, shard, *refs):
    parts, (sums_ref, keep_ref, send_ref, all_rows) = refs[:count], refs[count:]
    rows, width = shard.shape
    cond = 4 * rows
    at = parts[0].shape[1]
    fold = UNIT // rows
    te_at = pair.shape[1] - cond
    all_rows[0:2, :] = pair[...].astype(F32)
    all_rows[2:4, :] = got[...].astype(F32)
    sums_ref[:, :at] = sum(p[:UNIT, :].astype(F32) for p in parts).astype(BF)
    mods = all_rows[0:4, :width].astype(BF)
    te = all_rows[0:4, te_at:].astype(BF)
    lane = lax.broadcasted_iota(jnp.int32, (rows, cond), 1)
    pick = (lane == pos[0] * rows + lax.broadcasted_iota(jnp.int32, (rows, cond), 0)).astype(BF)
    te_own = mm(pick, te, NT).astype(BF)
    grad = mm(te_own, mods).astype(BF)
    part = width // fold
    for i in range(fold):
        sums_ref[i * rows : (i + 1) * rows, at : at + part] = grad[:, i * part : (i + 1) * part]
    at += part
    total = jnp.sum(all_rows[0:4, :te_at], axis=0, keepdims=True)
    sums_ref[:, at:] = jnp.zeros((UNIT, SMALL), BF)
    for i in range(te_at // SMALL):
        sums_ref[i : i + 1, at : at + SMALL] = total[:, i * SMALL : (i + 1) * SMALL].astype(BF)
    tg = mm(mods, shard[...], NT)
    keep_ref[...] = tg[0:2]
    send_ref[...] = tg[2:4]


def ada_part(pos, pair, got, shard, parts, after):
    rows, width = shard.shape
    out = (UNIT, parts[0].shape[1] + width * rows // UNIT + SMALL)
    args = (pair, got, shard, *parts)
    return call(
        partial(ada_kernel, len(parts)), pos, args, [once(a.shape) for a in args],
        [sds(out, BF), sds((2, rows), F32), sds((2, rows), F32)], [once(out), once((2, rows)), once((2, rows))], (1,),
        [pltpu.VMEM((4, pair.shape[1]), F32)], "ada_part", after,
    )


def unpack_kernel(plan, pos, *refs):
    half = UNIT // 2
    count = len(plan)
    outs = refs[2 * count :]
    for i, moves in enumerate(plan):
        for which, ref in enumerate(refs[2 * i : 2 * i + 2]):
            for out, row, col, at, width in moves:
                place = pos[1] ^ which
                if row is None:
                    outs[out][:, pl.ds(pl.multiple_of(place * width, 128), width)] = ref[:, at : at + width].astype(F32)
                    continue
                base = pl.multiple_of(row + place * half, half)
                outs[out][pl.ds(base, half), col : col + width] = ref[:, at : at + width].astype(F32)


def unpack(pos, plan, pairs, shapes, after):
    args = [a for pair in pairs for a in pair]
    return call(
        partial(unpack_kernel, plan), pos, args, [once(a.shape) for a in args],
        [sds(s, F32) for s in shapes], [once(s) for s in shapes], (1,), [], "unpack", after,
    )


def mlp_rest_kernel(units, span, pos, near, far, down_in, up_in, down, up):
    half = UNIT // 2
    width = down.shape[1]
    block, owner = pl.program_id(0), pl.program_id(1)
    for which, ref in enumerate((near, far)):
        place = pos[1] ^ which

        @pl.when(owner == 0)
        def _():
            for k in range(TILE // UNIT):
                base = pl.multiple_of(k * UNIT + place * half, half)
                at = pl.multiple_of((block * (TILE // UNIT) + k) * width, 128)
                down[pl.ds(base, half), :] = ref[:, pl.ds(at, width)].astype(F32)

        for k in range(units):
            base = pl.multiple_of(k * UNIT + place * half, half)
            at = pl.multiple_of(span // UNIT * width + (owner * units + k) * span + block * TILE, 128)
            up[pl.ds(base, half), :] = ref[:, pl.ds(at, TILE)].astype(F32)


def mlp_rest(pos, pair, down, up, start, span, after):
    afters = after if isinstance(after, tuple) else (after,)
    hidden, width = down.shape
    units = up.shape[0] // UNIT
    per, base = hidden // TILE, start // TILE
    anywhere = pl.BlockSpec(memory_space=pl.ANY)
    args = (*pair, down, up)
    return call(
        partial(mlp_rest_kernel, units, span), pos, args, [once(a.shape) for a in pair] + [anywhere] * 2,
        [sds(down.shape, F32), sds(up.shape, F32)],
        [
            pl.BlockSpec((TILE, width), lambda j, i, *_: (base + j, 0)),
            pl.BlockSpec((up.shape[0], TILE), lambda j, i, *_: (0, i * per + base + j)),
        ],
        (span // TILE, 4), [], "mlp_rest", afters, aliases={1 + len(afters) + 2: 0, 1 + len(afters) + 3: 1},
    )


def last_kernel(units, cols, ada_at, pos, near, far, qkv_in, qkv, ada, small):
    half = UNIT // 2
    part = pl.program_id(0)
    width = ada.shape[1] * ada.shape[0] // UNIT
    for which, ref in enumerate((near, far)):
        place = pos[1] ^ which
        for k in range(units):
            base = pl.multiple_of(k * UNIT + place * half, half)
            at = pl.multiple_of((3 * k + part) * cols, 128)
            qkv[pl.ds(base, half), :] = ref[:, pl.ds(at, cols)].astype(F32)

        @pl.when(part == 0)
        def _():
            ada[:, pl.ds(pl.multiple_of(place * width, 128), width)] = ref[:, ada_at : ada_at + width].astype(F32)
            small[pl.ds(pl.multiple_of(place * half, half), half), :] = ref[:, ada_at + width :].astype(F32)


def last_unpack(pos, pair, qkv, ada_shape, after):
    afters = after if isinstance(after, tuple) else (after,)
    quarter, wide = qkv.shape
    cols = HEADS_PER_STEP * HEAD_DIM
    units = quarter // UNIT
    small = (UNIT, SMALL)
    args = (*pair, qkv)
    return call(
        partial(last_kernel, units, cols, units * 3 * cols), pos, args,
        [once(a.shape) for a in pair] + [pl.BlockSpec(memory_space=pl.ANY)],
        [sds(qkv.shape, F32), sds(ada_shape, F32), sds(small, F32)],
        [pl.BlockSpec((quarter, cols), lambda i, *_: (0, i * (wide // 3 // cols))), whole(ada_shape), whole(small)],
        (3,), [], "last_unpack", afters, aliases={1 + len(afters) + 2: 0},
    )


ORDER = ("g1", "F2", "MB", "g1", "g2", "Bb", "g1", "g2", "qb", "Ba", "g1", "g2", "qb", "qa", "IB", "g1", "qb", "g2", "row", "qa", "tg", "g1", "qb", "qa", "g2", "qb", "qa", "U1", "g2", "qb", "qa", "U2", "qa", "UB")
ENDS = {"U1": "g1", "U2": "g2", "UB": "qb"}
ROW_FIRST = {"g1": True, "g2": True, "qb": True}
WIDE_FIRST = True


def rotary_tables(length):
    half = HEAD_DIM // 2
    frequency = 10000.0 ** (-2.0 * np.arange(half) / HEAD_DIM)
    angles = np.arange(length)[:, None] * frequency[None, :]
    cos, sin = np.cos(angles), np.sin(angles)
    table = lambda *parts: jnp.asarray(np.concatenate(parts, axis=1).astype(np.float32))
    return table(cos, cos, cos, cos), table(-sin, sin, -sin, sin)


def local(
    mesh, block_input, cotangent, time_embed, ada_weight, ada_bias, attn_gain, qkv_weight, out_weight,
    mlp_gain, up_weight, up_bias, down_weight, down_bias,
):
    net = Net(mesh)
    length, width = block_input.shape
    f = net.f
    pos = jnp.stack([f] + [(net.d // bit) % 2 for bit in bits_of(net.dp)]).astype(jnp.int32)
    cond = time_embed.shape[1]
    quarter = width // 4
    ada_rows = ada_weight.shape[0]
    hidden_quarter = down_weight.shape[0]
    third = hidden_quarter // 3
    start_1, one = (0, 2 * third) if WIDE_FIRST else (2 * third, third)
    start_2, two = (2 * third, third) if WIDE_FIRST else (0, 2 * third)
    cols = HEADS_PER_STEP * HEAD_DIM
    groups = width // cols
    w = width
    cos, sin = rotary_tables(length)
    by_seq = lambda rel: jnp.take(rel, jnp.arange(4) ^ f, axis=0)

    units = quarter // UNIT
    in_groups = lambda a, b: [
        (0, k * UNIT, part * w + j * cols, cols) for k in range(units) for j in range(a, b) for part in range(3)
    ]
    of_up = lambda start, size: [
        (0, k * UNIT, i * hidden_quarter + start, size) for k in range(units) for i in range(4)
    ]
    of_down = lambda start, size: [(2, start + k * UNIT, 0, w) for k in range(size // UNIT)]
    rows = lambda v, at, n: lax.dynamic_slice_in_dim(v, at, n, 0)
    far_of = lambda near, far: (near, far, net.core_swap(near), net.core_swap(far))

    te_got = net.core_swap(time_embed)
    half_a, half_b = pack_halves(pos, [in_groups(0, 1), in_groups(1, groups)], [qkv_weight])
    half_a, attn_gain = tie(half_a, attn_gain)
    te = jnp.concatenate([time_embed, te_got], axis=0)
    te, half_b, attn_gain = tie(te, half_b, attn_gain)
    smalls = (attn_gain, mlp_gain, down_bias, up_bias, ada_bias)
    small = jnp.concatenate(smalls).reshape(1, -1)
    small_got = net.core_swap(small)
    te = jnp.concatenate([te, net.row_swap(te)], axis=0)
    near_a = net.row_swap(half_a)
    part = jnp.dot(
        lax.dynamic_slice_in_dim(by_seq(te), f * ada_rows, ada_rows, 1), ada_weight, preferred_element_type=F32
    )
    part_send = rows(part, 2 * (1 - net.row), 2)
    part_got = net.row_swap(part_send)
    small = jnp.concatenate([small, small_got], axis=0)
    small_far = net.row_swap(small)
    near_b = net.row_swap(half_b)
    partner_qkv = net.core_swap(qkv_weight)
    far_a = net.dp_swap(near_a, 1)
    up_weight, out_weight, down_weight, part_send = tie(up_weight, out_weight, down_weight, part_send)
    half_1, half_2, half_3 = pack_halves(
        pos,
        [
            of_up(start_1, one) + [(1, k * UNIT, 0, w) for k in range(units)], of_down(start_1, one),
            of_up(start_2, two) + of_down(start_2, two),
        ],
        [up_weight, out_weight, down_weight],
    )
    far_a = far_of(near_a, far_a)
    small = by_seq(jnp.concatenate([small, small_far], axis=0))
    part = rows(part, 2 * net.row, 2) + part_got
    cuts = np.cumsum([0] + [v.shape[0] for v in smalls])
    gain_a, gain_m, bias_d, bias_u, bias_ada = (
        small[:, cuts[i] : cuts[i + 1]].astype(F32).reshape(1, -1) for i in range(5)
    )
    mod = rows(part, net.core, 1) + net.core_swap(rows(part, 1 - net.core, 1)) + bias_ada
    near_b, block_input = tie(near_b, block_input)
    far_b = net.dp_swap(near_b, 1)
    near_1, near_2, near_3 = (net.row_swap(v) for v in (half_1, half_2, half_3))
    partner_out, partner_up, partner_down = (net.core_swap(v) for v in (out_weight, up_weight, down_weight))

    attn_in, *saved_a = attention_forward(
        pos, 0, 1, True, block_input, gain_a, mod, (qkv_weight, partner_qkv, *far_a), cos, sin
    )
    far_b, near_1, attn_in = tie(far_b, near_1, attn_in)
    far_b = far_of(near_b, far_b)
    far_1 = net.dp_swap(near_1, 1)
    saved_b = attention_forward(
        pos, 1, groups - 1, False, attn_in, gain_a, mod, (qkv_weight, partner_qkv, *far_b), cos, sin
    )
    if WIDE_FIRST:
        far_1, near_2, o_b = tie(far_1, near_2, saved_b[4])
    else:
        far_1, near_2, near_3, o_b = tie(far_1, near_2, near_3, saved_b[4])
    far_1 = far_of(near_1, far_1)
    far_2 = net.dp_swap(near_2, 1)
    os = (saved_a[4], o_b)
    branch, middle, mlp_in, mlp_grad, out_full = middle_forward(
        pos, os, block_input, cotangent, mod, gain_m, out_weight, partner_out, far_1, units * 4 * one
    )
    far_2, near_3, mlp_in = tie(far_2, near_3, mlp_in)
    far_2 = far_of(near_2, far_2)
    far_3 = net.dp_swap(near_3, 1)
    mb, back, bias_g1, *s1 = mlp(
        pos, mlp_in, mlp_grad, bias_u, (up_weight, partner_up, *far_1), (down_weight, partner_down, *far_2), 0,
        start_1, one, None, True,
    )
    far_3, mb, *s1 = tie(far_3, mb, *s1)
    far_3 = far_of(near_3, far_3)
    chunks = {"g1": Chunk(net, s1, ROW_FIRST["g1"])}
    state = {}

    def run(name, after):
        if name == "F2":
            mb2, back2, state["bias_g2"], *s2 = mlp(
                pos, mlp_in, mlp_grad, bias_u, (up_weight, partner_up, *far_3), (down_weight, partner_down, *far_3),
                units * 4 * two, start_2, two, (mb, back), True, after,
            )
            chunks["g2"] = Chunk(net, s2, ROW_FIRST["g2"])
            state["mb"], state["back"] = mb2, back2
            return back2
        if name == "MB":
            state["mid"], state["out"], state["low"], state["do"], state["sums_m"] = middle_back(
                pos, state["back"], state["mb"], middle, branch, cotangent, mod, gain_m, bias_d, out_full, after
            )
            return state["do"]
        if name == "Bb":
            state["grad_b"], *sb = attention_back(
                pos, saved_b, state["do"], cols, attn_in, cos, sin, (os, state["low"]), after
            )
            chunks["qb"] = Chunk(net, sb, ROW_FIRST["qb"])
            return state["grad_b"]
        if name == "Ba":
            state["grad_a"], *sa = attention_back(pos, saved_a, state["do"], 0, attn_in, cos, sin, None, after)
            chunks["qa"] = Chunk(net, sa, True, extend)
            return state["grad_a"]
        if name == "IB":
            state["input_grad"], row = input_back(
                pos, (state["grad_a"], state["grad_b"]), (0, 1), (qkv_weight, partner_qkv, *far_a, *far_b),
                block_input, state["mid"], mod, gain_a, state["sums_m"], time_embed, (bias_g1, state["bias_g2"]) if WIDE_FIRST else (state["bias_g2"], bias_g1), after,
            )
            state["row"], state["row_got"] = row, net.core_swap(row)
            return state["input_grad"]
        if name == "row":
            state["pair"] = jnp.concatenate([*follow(after, state["row"]), state["row_got"]], axis=0)
            state["pair_got"] = net.row_swap(state["pair"])
            return state["pair"]
        if name == "tg":
            keep, = follow(after, state["tg_keep"])
            state["give"] = jnp.concatenate([keep[1:2], state["tg_got"][1:2]], axis=0)
            state["given"] = net.core_swap(state["give"])
            return state["give"]
        if name == "U1":
            plan = [(0, start_1 + k * UNIT, 0, k * w, w) for k in range(one // UNIT)] + [
                (1, k * UNIT, i * hidden_quarter + start_1, one // UNIT * w + (i * units + k) * one, one)
                for i in range(4) for k in range(units)
            ]
            state["down_grad"], state["up_grad"] = unpack(
                pos, [plan], [chunks["g1"].ready], ((hidden_quarter, w), (quarter, 4 * hidden_quarter)), after
            )
            return state["up_grad"]
        if name == "UB":
            wide = units * 3 * cols
            plan = [
                (0, k * UNIT, part_ * w + j * cols, (j - 1) * wide + k * 3 * cols + part_ * cols, cols)
                for j in range(1, groups) for k in range(units) for part_ in range(3)
            ] + [(1, k * UNIT, 0, (groups - 1) * wide + k * w, w) for k in range(units)]
            state["qkv_grad"], state["out_grad"] = unpack(
                pos, [plan], [chunks["qb"].ready], ((quarter, 3 * w), (quarter, w)), after
            )
            return state["out_grad"]
        if name == "U2":
            state["down_grad"], state["up_grad"] = mlp_rest(
                pos, chunks["g2"].ready, state["down_grad"], state["up_grad"], start_2, two, after
            )
            return state["up_grad"]
        return chunks[name].step(after)

    def extend(parts, after):
        merged, state["tg_keep"], state["tg_send"] = ada_part(
            pos, state["pair"], state["pair_got"], ada_weight, [p.base for p in parts], after
        )
        state["tg_got"] = net.row_swap(state["tg_send"])
        return merged

    def finish(names, after):
        while any(chunks[n].where != "end" for n in names):
            for n in names:
                if chunks[n].where != "end":
                    after = run(n, after)
        return after

    after = None
    for name in ORDER:
        if name in chunks and chunks[name].where == "end":
            continue
        if name in ENDS:
            after = finish([ENDS[name]], after)
        after = run(name, after)
    after = finish(["qa"], after)

    block_output, input_grad = state["out"], state["input_grad"]
    down_grad, up_grad = state["down_grad"], state["up_grad"]
    qkv_grad, ada_weight_grad, small_sums = last_unpack(
        pos, chunks["qa"].ready, state["qkv_grad"], ada_weight.shape, after
    )
    out_grad = state["out_grad"]
    total = small_sums.reshape(-1)
    own_cols = lambda start, size: lax.dynamic_slice_in_dim(total, start + f * size, size, 0)
    ada_bias_grad = own_cols(0, 6 * w // 4)
    attn_gain_grad = own_cols(6 * w, quarter)
    mlp_gain_grad = own_cols(7 * w, quarter)
    down_bias_grad = own_cols(8 * w, quarter)
    up_bias_grad = own_cols(9 * w, up_bias.shape[0])
    tg_keep, tg_got, given = state["tg_keep"], state["tg_got"], state["given"]
    parts = jnp.concatenate([tg_keep[0:1], given[0:1], tg_got[0:1], given[1:2]], axis=0)
    time_grad = by_seq(parts).reshape(1, cond)
    return (
        block_output, input_grad, time_grad, ada_weight_grad, ada_bias_grad, attn_gain_grad, qkv_grad, out_grad,
        mlp_gain_grad, up_grad, up_bias_grad, down_grad, down_bias_grad,
    )


def solution(mesh):
    rows, shard, line = P(("dp", "fsdp"), None), P("fsdp", None), P("fsdp")
    return jax.shard_map(
        partial(local, mesh),
        mesh=mesh,
        in_specs=(rows, rows, rows, shard, line, line, shard, shard, line, shard, line, shard, line),
        out_specs=(rows, rows, rows, shard, line, line, shard, shard, line, shard, line, shard, line),
        check_vma=False,
    )
```

```python
from functools import partial

import numpy as np

import jax
import jax.numpy as jnp
from jax import lax
from jax.experimental import pallas as pl
from jax.experimental.pallas import tpu as pltpu
from jax.sharding import PartitionSpec as P

HEAD_DIM = 64
BF = jnp.bfloat16
F32 = jnp.float32
NN = (((1,), (0,)), ((), ()))
NT = (((1,), (1,)), ((), ()))
TN = (((0,), (0,)), ((), ()))
VMEM_LIMIT = 60 * 2**20
HEADS_PER_STEP = 4
GELU_C = 0.7978845608028654
GELU_A = 0.044715


def mm(a, b, dims=NN):
    return lax.dot_general(a, b, dims, preferred_element_type=F32)


UNIT = 64


def swap(value, axis, size, bit):
    return lax.ppermute(value, axis, [(i, i ^ bit) for i in range(size)])


def bits_of(size):
    bits, bit = [], 1
    while bit < size:
        bits.append(bit)
        bit *= 2
    return bits


def tie(*values):
    return lax.optimization_barrier(values)


class Net:
    def __init__(self, mesh):
        self.dp = mesh.shape["dp"]
        self.fsdp = mesh.shape["fsdp"]
        self.d = lax.axis_index("dp")
        self.f = lax.axis_index("fsdp")
        self.core = self.f % 2
        self.row = self.f // 2
        self.side = self.d % 2
        self.zero = self.d // self.dp

    def core_swap(self, v):
        return swap(v, "fsdp", self.fsdp, 1)

    def row_swap(self, v):
        return swap(v, "fsdp", self.fsdp, 2)

    def dp_swap(self, v, bit):
        return swap(v, "dp", self.dp, bit)


def follow(after, *values):
    if after is None:
        return list(values)
    return list(tie(after, *values)[1:])


class Part:
    def __init__(self, base, cuts=()):
        self.base, self.cuts = base, cuts

    def cut(self, which):
        return Part(self.base, self.cuts + (which,))

    def read(self):
        v = self.base
        for which in self.cuts:
            half = v.shape[0] // 2
            v = lax.dynamic_slice_in_dim(v, which * half, half, 0)
        return v.astype(F32)


def add(parts):
    return sum(p.read() for p in parts).astype(BF)


def hold(after, parts):
    bases = []
    for p in parts:
        if not any(p.base is b for b in bases):
            bases.append(p.base)
    held = follow(after, *bases)
    return [Part(next(h for h, b in zip(held, bases) if b is p.base), p.cuts) for p in parts]


def chunk_steps(net, keep, send, row_first, extend):
    got, after = yield ("core", send)
    kept = Part(*follow(after, keep))
    came = Part(got)
    near, far = [kept.cut(net.zero), came.cut(net.zero)], [kept.cut(1 + net.zero), came.cut(1 + net.zero)]
    bits = bits_of(net.dp)
    todo = (["row"] + bits[:-1]) if row_first else (bits[:1] + ["row"] + bits[1:-1])
    split = True
    for where in todo:
        if where == "row":
            got, after = yield (where, add(far))
            near = hold(after, near) + [Part(got)]
            split = False
            if extend:
                near = [Part(extend(near, after))]
            continue
        which = (net.d // where) % 2
        give = lambda parts: add([p.cut(1 - which) for p in parts])
        stay = lambda parts: [p.cut(which) for p in parts]
        if split:
            (near_got, far_got), after = yield (where, tie(give(near), give(far)))
            both = hold(after, near + far)
            near, far = stay(both[: len(near)]) + [Part(near_got)], stay(both[len(near) :]) + [Part(far_got)]
        else:
            got, after = yield (where, give(near))
            near = stay(hold(after, near)) + [Part(got)]
    own = add(near)
    got, after = yield (bits[-1], own)
    total = add(hold(after, [Part(own)]) + [Part(got)])
    for bit in reversed(bits[:-1]):
        got, after = yield (bit, total)
        if bit != 1:
            first = (net.d // bit) % 2 == 0
            (total,) = follow(after, total)
            total = jnp.concatenate([jnp.where(first, total, got), jnp.where(first, got, total)], axis=0)
    yield ("end", (total, got))


class Chunk:
    def __init__(self, net, shares, row_first=True, extend=None):
        self.net = net
        self.steps = chunk_steps(net, *shares, row_first, extend)
        self.where, self.ready = next(self.steps)
        self.got = net.core_swap(self.ready)

    def step(self, after):
        self.where, self.ready = self.steps.send((self.got, after))
        if self.where == "end":
            return after
        if self.where == "row":
            self.got = self.net.row_swap(self.ready)
        elif isinstance(self.ready, (list, tuple)):
            self.got = [self.net.dp_swap(v, self.where) for v in self.ready]
            return self.ready[0]
        else:
            self.got = self.net.dp_swap(self.ready, self.where)
        return self.ready


def normed(values):
    centre = jnp.mean(values, axis=-1, keepdims=True)
    centred = values - centre
    spread = jnp.mean(centred * centred, axis=-1, keepdims=True)
    r = lax.rsqrt(spread + 1e-05)
    return centred * r, r


def norm_back(grad, n, r, gain, scale):
    e = grad * (1.0 + scale) * gain
    return r * (e - jnp.mean(e, -1, keepdims=True) - n * jnp.mean(e * n, -1, keepdims=True))


def column_sum(v):
    return jnp.sum(v, axis=0, keepdims=True)


def of_head(shape, head):
    return (lax.broadcasted_iota(jnp.int32, shape, 1) // HEAD_DIM) == head


def turn(v, cos, sin):
    half = HEAD_DIM // 2
    low = (lax.broadcasted_iota(jnp.int32, v.shape, 1) // half) % 2 == 0
    width = v.shape[1]
    other = jnp.where(low, pltpu.roll(v, width - half, 1), pltpu.roll(v, half, 1))
    return v * cos + other * sin


def place_near(full, pos, own, partner, cols=((0, 0, None),)):
    rows = own.shape[0]
    for ref, flip in ((own, 0), (partner, 1)):
        base = pl.multiple_of((pos[0] ^ flip) * rows, UNIT)
        for to, at, width in cols:
            width = width or full.shape[1]
            full[pl.ds(base, rows), to : to + width] = ref[:, at : at + width]


def place_far(full, pos, far, rows, at, width):
    half = UNIT // 2
    for i, ref in enumerate(far):
        for k in range(rows // UNIT):
            base = pl.multiple_of((pos[0] ^ (2 + i // 2)) * rows + k * UNIT + (pos[1] ^ (i % 2)) * half, half)
            full[pl.ds(base, half), :] = ref[:, at + k * width : at + (k + 1) * width]


def store_shares(pos, grad, shares, at):
    quarter, width = grad.shape[0] // 4, grad.shape[1]
    for owner in range(4):
        rel = pos[0] ^ owner
        blocks = [
            grad[owner * quarter + k * UNIT : owner * quarter + (k + 1) * UNIT].astype(BF)
            for k in range(quarter // UNIT)
        ]
        put_shares(rel, blocks, shares, at)


def put_shares(rel, blocks, shares, at):
    row = pl.multiple_of(rel // 2 * UNIT, UNIT)

    def put(ref):
        for k, block in enumerate(blocks):
            ref[pl.ds(row, UNIT), at(k, block.shape[1])] = block

    for index in range(2):
        pl.when(rel % 2 == index)(partial(put, shares[index]))


def pack_kernel(plan, pos, *refs):
    half = UNIT // 2
    outs = refs[len(refs) - len(plan) :]
    for out, moves in zip(outs, plan):
        to = 0
        for src, row, col, width in moves:
            base = pl.multiple_of(row + pos[1] * half, half)
            out[:, to : to + width] = refs[src][pl.ds(base, half), col : col + width]
            to += width


def pack_halves(pos, plan, arrays):
    outs = [sds((UNIT // 2, sum(m[3] for m in moves)), BF) for moves in plan]
    return call(
        partial(pack_kernel, plan), pos, arrays, [once(a.shape) for a in arrays], outs, [once(o.shape) for o in outs],
        (1,), [], "pack_halves", cost=10,
    )


def attention_kernel(group, first, pos, x_ref, gain_ref, mod_ref, own, partner, n0, n1, n2, n3, cos_ref, sin_ref, *rest):
    if first:
        in_ref, q_ref, k_ref, v_ref, p_ref, o_ref, full = rest
    else:
        q_ref, k_ref, v_ref, p_ref, o_ref, full = rest
        in_ref = x_ref
    cols = q_ref.shape[1]
    step = pl.program_id(0)
    width = x_ref.shape[1]

    @pl.when(step == 0)
    def _():
        place_groups(full, pos, own, partner, (n0, n1, n2, n3), group, cols)
        if first:
            n, _ = normed(x_ref[...].astype(F32))
            shift, scale = mod_ref[:, :width], mod_ref[:, width : 2 * width]
            in_ref[...] = (n * gain_ref[...] * (1.0 + scale) + shift).astype(BF)

    base = pl.multiple_of(step * 3 * cols, cols)
    attn_in = in_ref[...]
    cos, sin = cos_ref[...], sin_ref[...]
    q_all = mm(attn_in, full[:, pl.ds(base, cols)])
    k_all = mm(attn_in, full[:, pl.ds(base + cols, cols)])
    v_ref[...] = mm(attn_in, full[:, pl.ds(base + 2 * cols, cols)]).astype(BF)
    for pair in range(cols // 128):
        sl = slice(pair * 128, pair * 128 + 128)
        q = turn(q_all[:, sl], cos, sin).astype(BF) * BF(HEAD_DIM**-0.5)
        k = turn(k_all[:, sl], cos, sin).astype(BF)
        q_ref[:, sl] = q
        k_ref[:, sl] = k
        v = v_ref[:, sl]
        outs = []
        for h in range(2):
            kh = jnp.where(of_head(k.shape, h), k, jnp.zeros_like(k))
            s = mm(kh, q, NT)
            e = jnp.exp(s - jnp.max(s, axis=0, keepdims=True))
            p = (e * (1.0 / jnp.sum(e, axis=0, keepdims=True))).astype(BF)
            p_ref[2 * pair + h] = p
            outs.append(mm(p, v, TN))
        o_ref[:, sl] = jnp.where(of_head(outs[0].shape, 0), outs[0], outs[1]).astype(BF)


def whole(shape):
    return pl.BlockSpec(shape, lambda *_: (0,) * len(shape))


def once(shape):
    return pl.BlockSpec(shape, lambda *_: (0,) * len(shape), pipeline_mode=pl.Buffered(1))


def place_groups(full, pos, own, partner, far, group, cols):
    width = own.shape[1] // 3
    moves = [
        ((3 * j + part) * cols, part * width + (group + j) * cols, cols)
        for j in range(full.shape[1] // (3 * cols)) for part in range(3)
    ]
    place_near(full, pos, own, partner, moves)
    place_far(full, pos, far, own.shape[0], 0, full.shape[1])


def sds(shape, dtype):
    return jax.ShapeDtypeStruct(shape, dtype)


def call(body, pos, args, in_specs, outs, out_specs, grid, scratch, name, after=None, cost=0, aliases={}):
    if after is not None:
        inner, afters = body, after if isinstance(after, tuple) else (after,)
        body = lambda pos_ref, *refs: inner(pos_ref, *refs[len(afters) :])
        args, in_specs = (*afters, *args), [pl.BlockSpec(memory_space=pl.ANY)] * len(afters) + [*in_specs]
    return pl.pallas_call(
        body,
        grid_spec=pltpu.PrefetchScalarGridSpec(
            num_scalar_prefetch=1, grid=grid, in_specs=in_specs, out_specs=out_specs, scratch_shapes=scratch
        ),
        out_shape=outs,
        compiler_params=pltpu.CompilerParams(vmem_limit_bytes=VMEM_LIMIT),
        cost_estimate=pl.CostEstimate(flops=1024 + cost * 10**9, bytes_accessed=1024, transcendentals=0),
        input_output_aliases=aliases,
        name=name,
    )(pos, *args)


def attention_forward(pos, group, count, first, x, gain, mod, pieces, cos, sin):
    length, width = x.shape
    cols = HEADS_PER_STEP * HEAD_DIM
    row = pl.BlockSpec((length, cols), lambda j, *_: (0, j))
    args = (x, gain, mod, *pieces, cos, sin)
    qkv_out = sds((length, count * cols), BF)
    outs = [qkv_out] * 3 + [sds((count * HEADS_PER_STEP, length, length), BF), qkv_out]
    specs = [row, row, row, pl.BlockSpec((HEADS_PER_STEP, length, length), lambda j, *_: (j, 0, 0)), row]
    if first:
        outs, specs = [sds(x.shape, BF)] + outs, [whole(x.shape)] + specs
    return call(
        partial(attention_kernel, group, first), pos, args, [once(a.shape) for a in args], outs, specs,
        (count,), [pltpu.VMEM((width, count * 3 * cols), BF)], "attention_forward", cost=30,
    )


ROWS = 192


def rows_of(shape):
    return pl.BlockSpec((ROWS, shape[1]), lambda i, *_: (i, 0))


def middle_kernel(count, units, pos, *refs):
    o_refs, refs = refs[:count], refs[count:]
    x_ref, g_ref, mod_ref, gain_ref, own, partner, *far = refs[: 6 + 4 * units]
    branch_ref, middle_ref, in_ref, grad_ref, full = refs[6 + 4 * units :]
    width = x_ref.shape[1]
    half = UNIT // 2

    @pl.when(pl.program_id(0) == 0)
    def _():
        place_near(full, pos, own, partner)
        for i in range(4):
            for k in range(units):
                base = (pos[0] ^ (2 + i // 2)) * own.shape[0] + k * UNIT + (pos[1] ^ (i % 2)) * half
                full[pl.ds(pl.multiple_of(base, half), half), :] = far[i * units + k][...]

    piece = lambda i: mod_ref[:, i * width : (i + 1) * width]
    branch, at = jnp.zeros(x_ref.shape, F32), 0
    for o_ref in o_refs:
        branch += mm(o_ref[...], full[at : at + o_ref.shape[1], :])
        at += o_ref.shape[1]
    branch_ref[...] = branch
    middle = x_ref[...].astype(F32) + piece(2) * branch
    middle_ref[...] = middle
    n, _ = normed(middle)
    in_ref[...] = (n * gain_ref[...] * (1.0 + piece(4)) + piece(3)).astype(BF)
    grad_ref[...] = (piece(5) * g_ref[...].astype(F32)).astype(BF)


def middle_forward(pos, os, x, g, mod, gain, own, partner, far, at):
    length, width = x.shape
    units = own.shape[0] // UNIT
    args = (*os, x, g, mod, gain, own, partner, *[p for p in far for _ in range(units)])
    specs = [rows_of(a.shape) for a in (*os, x, g)] + [once(a.shape) for a in (mod, gain, own, partner)]
    specs += [
        pl.BlockSpec((UNIT // 2, width), lambda *_, k=k: (0, at // width + k), pipeline_mode=pl.Buffered(1))
        for _ in far for k in range(units)
    ]
    full = sds((width, width), BF)
    return call(
        partial(middle_kernel, len(os), units), pos, args, specs,
        [sds(x.shape, F32), sds(x.shape, F32), sds(x.shape, BF), sds(x.shape, BF), full],
        [rows_of(x.shape)] * 4 + [whole(full.shape)], (length // ROWS,), [], "middle_forward", cost=30,
    )


TILE = 256


def mlp_kernel(start, span, first, joint, down_at, pos, *refs):
    tiles = span // TILE
    refs = list(refs)
    take = lambda n: [refs.pop(0) for _ in range(n)]
    in_ref, grad_ref, bias_ref = take(3)
    own_up, partner_up = take(tiles), take(tiles)
    units = own_up[0].shape[0] // UNIT
    far_up = [take(units) for _ in range(4)]
    own_down, partner_down, *far_down = take(6)
    if not first:
        branch_in, back_in = take(2)
    branch_ref, back_ref, bias_grad_ref = take(3)
    shares_d = take(2)
    shares_u = shares_d if joint else take(2)
    up, down = refs
    step = pl.program_id(0)
    hidden = 4 * own_down.shape[0]
    rows = own_up[0].shape[0]
    half = UNIT // 2
    f, side = pos[0], pos[1]

    @pl.when(step == 0)
    def _():
        if first:
            branch_ref[...] = jnp.zeros_like(branch_ref)
            back_ref[...] = jnp.zeros_like(back_ref)
        else:
            branch_ref[...] = branch_in[...]
            back_ref[...] = back_in[...]

    for many, flip in ((own_up, 0), (partner_up, 1)):
        base = pl.multiple_of((f ^ flip) * rows, UNIT)
        for i, ref in enumerate(many):
            up[pl.ds(base, rows), i * TILE : (i + 1) * TILE] = ref[...]
    for i, many in enumerate(far_up):
        for k, ref in enumerate(many):
            base = pl.multiple_of((f ^ (2 + i // 2)) * rows + k * UNIT + (side ^ (i % 2)) * half, half)
            up[pl.ds(base, half), :] = ref[...]

    rel = f ^ step
    width = in_ref.shape[1]
    for index, ref in ((0, own_down), (1, partner_down)):

        @pl.when(rel == index)
        def _():
            down[...] = ref[start : start + span, :]

    for index, pair in ((2, far_down[:2]), (3, far_down[2:])):

        @pl.when(rel == index)
        def _():
            for h, ref in enumerate(pair):
                for k in range(span // UNIT):
                    base = pl.multiple_of(k * UNIT + (side ^ h) * half, half)
                    down[pl.ds(base, half), :] = ref[:, down_at + k * width : down_at + (k + 1) * width]

    mlp_in, mlp_grad = in_ref[...], grad_ref[...]
    up_t, down_t = up[...], down[...]
    base = pl.multiple_of(step * (hidden // 4) + start, 128)
    pre = mm(mlp_in, up_t) + bias_ref[:, pl.ds(base, span)]
    t = jnp.tanh(GELU_C * (pre + GELU_A * (pre * pre * pre)))
    activ = (0.5 * pre * (1.0 + t)).astype(BF)
    slope = 0.5 * (1.0 + t) + (0.5 * GELU_C) * pre * (1.0 - t * t) * (1.0 + (3.0 * GELU_A) * (pre * pre))
    pre_grad = (mm(mlp_grad, down_t, NT) * slope).astype(BF)
    bias_grad_ref[:, pl.ds(pl.multiple_of(step * span, span), span)] = column_sum(pre_grad.astype(F32))
    branch_ref[...] += mm(activ, down_t)
    back_ref[...] += mm(pre_grad, up_t, NT)
    dd = mm(activ, mlp_grad, TN).astype(BF)
    put_shares(rel, [dd[k * UNIT : (k + 1) * UNIT] for k in range(span // UNIT)], shares_d, lambda k, w: slice(k * w, (k + 1) * w))
    after = (span // UNIT) * width if joint else 0
    at = lambda k, w: pl.ds(pl.multiple_of(after + (step * units + k) * w, 128), w)
    store_shares(pos, mm(mlp_in, pre_grad, TN), shares_u, at)


def mlp(pos, mlp_in, mlp_grad, bias, ups, downs, down_at, start, span, carried, joint, after=None):
    length, width = mlp_in.shape
    first = carried is None
    rows, hidden = ups[0].shape
    tiles, units, per = span // TILE, rows // UNIT, hidden // 4 // TILE
    args = [mlp_in, mlp_grad, bias]
    specs = [once(a.shape) for a in args]
    for ref in ups[:2]:
        for i in range(tiles):
            args.append(ref)
            specs.append(pl.BlockSpec((rows, TILE), lambda s, *_, i=i: (0, s * per + start // TILE + i)))
    for ref in ups[2:]:
        for k in range(units):
            args.append(ref)
            specs.append(pl.BlockSpec((UNIT // 2, span), lambda s, *_, k=k: (0, k * 4 + s)))
    args += list(downs)
    specs += [once(a.shape) for a in downs]
    if not first:
        args += list(carried)
        specs += [once(a.shape) for a in carried]
    acc = sds((length, width), F32)
    cols_d, cols_u = (span // UNIT) * width, 4 * units * span
    shares = [sds((2 * UNIT, c), BF) for c in ((cols_d + cols_u,) if joint else (cols_d, cols_u)) for _ in range(2)]
    return call(
        partial(mlp_kernel, start, span, first, joint, down_at), pos, args, specs,
        [acc, acc, sds((1, 4 * span), F32), *shares],
        [once((length, width))] * 2 + [once((1, 4 * span))] + [once(v.shape) for v in shares],
        (4,), [pltpu.VMEM((width, span), BF), pltpu.VMEM((span, width), BF)], "mlp_first" if first else "mlp_second", after,
        60 if first else 0,
    )


def add_sums(ref, sums):
    @pl.when(pl.program_id(0) == 0)
    def _():
        ref[...] = jnp.zeros_like(ref)

    for i, v in enumerate(sums):
        width = v.shape[1]
        ref[:, i * width : (i + 1) * width] += v


def middle_back_kernel(
    pos, back_ref, mlp_ref, middle_ref, branch_ref, g_ref, mod_ref, gain_ref, bias_ref, out_w,
    grad_ref, out_ref, low_ref, do_ref, sums_ref,
):
    width = g_ref.shape[1]
    piece = lambda i: mod_ref[:, i * width : (i + 1) * width]
    g = g_ref[...].astype(F32)
    middle = middle_ref[...]
    branch = branch_ref[...]
    gain = gain_ref[...]
    mlp_branch = mlp_ref[...] + bias_ref[...]
    out_ref[...] = (middle + piece(5) * mlp_branch).astype(BF)
    n, r = normed(middle)
    back = back_ref[...]
    back_sum = column_sum(back * n)
    grad = g + norm_back(back, n, r, gain, piece(4))
    grad_ref[...] = grad
    low = (piece(2) * grad).astype(BF)
    low_ref[...] = low
    sums = (
        column_sum(grad * branch),
        column_sum(back),
        back_sum * gain,
        column_sum(g * mlp_branch),
        back_sum * (1.0 + piece(4)),
        column_sum((piece(5) * g).astype(BF).astype(F32)),
    )
    add_sums(sums_ref, sums)
    do_ref[...] = mm(low, out_w[...], NT).astype(BF)


def middle_back(pos, back, mlp_branch, middle, branch, g, mod, gain, bias, out_w, after):
    length, width = g.shape
    args = (back, mlp_branch, middle, branch, g, mod, gain, bias, out_w)
    return call(
        middle_back_kernel, pos, args, [rows_of(a.shape) for a in args[:5]] + [once(a.shape) for a in args[5:]],
        [sds(g.shape, F32), sds(g.shape, BF), sds(g.shape, BF), sds(g.shape, BF), sds((1, 6 * width), F32)],
        [rows_of(g.shape)] * 4 + [whole((1, 6 * width))], (length // ROWS,), [], "middle_back", after, 60,
    )


def attention_back_kernel(extra, groups, pos, q_ref, k_ref, v_ref, p_ref, o_ref, do_ref, in_ref, cos_ref, sin_ref, *rest):
    rest = list(rest)
    if extra:
        o_all = [rest.pop(0) for _ in range(extra)]
        low_ref = rest.pop(0)
    grad_ref, *shares = rest
    cols = q_ref.shape[1]
    at = lambda k, w: slice(k * w, (k + 1) * w)

    def heads():
        cos, sin = cos_ref[...], -sin_ref[...]
        for pair in range(cols // 128):
            sl = slice(pair * 128, pair * 128 + 128)
            q, k, v, do = q_ref[:, sl], k_ref[:, sl], v_ref[:, sl], do_ref[:, sl]
            od = o_ref[:, sl].astype(F32) * do.astype(F32)
            dq, dk, dv = [], [], []
            for h in range(2):
                mask = of_head(v.shape, h)
                p = p_ref[2 * pair + h]
                dp = mm(jnp.where(mask, v, jnp.zeros_like(v)), do, NT)
                delta = jnp.sum(jnp.where(mask, od, 0.0).T, axis=0, keepdims=True)
                ds = (p.astype(F32) * (dp - delta)).astype(BF)
                dv.append(mm(p, do))
                dk.append(mm(ds, q))
                dq.append(mm(ds, k, TN))
            mask = of_head(q.shape, 0)
            both = lambda pair_: jnp.where(mask, pair_[0], pair_[1])
            grad_ref[:, sl] = turn(both(dq) * HEAD_DIM**-0.5, cos, sin).astype(BF)
            grad_ref[:, cols + pair * 128 : cols + pair * 128 + 128] = turn(both(dk), cos, sin).astype(BF)
            grad_ref[:, 2 * cols + pair * 128 : 2 * cols + pair * 128 + 128] = both(dv).astype(BF)
        store_shares(pos, mm(in_ref[...], grad_ref[...], TN), shares, at)

    if not extra:
        heads()
        return
    step = pl.program_id(0)
    pl.when(step < groups)(heads)

    @pl.when(step == groups)
    def _():
        low = low_ref[...]
        parts = [mm(o_[...], low, TN) for o_ in o_all]
        store_shares(pos, jnp.concatenate(parts, axis=0), shares, at)


def attention_back(pos, saved, do, do_at, attn_in, cos, sin, extra, after):
    q, k, v, p, o = saved
    length, width = attn_in.shape
    cols = HEADS_PER_STEP * HEAD_DIM
    groups = q.shape[1] // cols
    last = groups - 1
    row = pl.BlockSpec((length, cols), lambda j, *_: (0, jnp.minimum(j, last)))
    do_row = pl.BlockSpec((length, cols), lambda j, *_: (0, do_at // cols + jnp.minimum(j, last)))
    steps = groups + (1 if extra else 0)
    share = sds((2 * UNIT, steps * width // 4 // UNIT * 3 * cols), BF)
    share_spec = pl.BlockSpec((2 * UNIT, width // 4 // UNIT * 3 * cols), lambda j, *_: (0, j))
    args = [q, k, v, p, o, do, attn_in, cos, sin]
    specs = [row, row, row, pl.BlockSpec((HEADS_PER_STEP, length, length), lambda j, *_: (jnp.minimum(j, last), 0, 0)),
             row, do_row, once(attn_in.shape), once(cos.shape), once(sin.shape)]
    if extra:
        args += [*extra[0], extra[1]]
        specs += [once(a.shape) for a in (*extra[0], extra[1])]
    return call(
        partial(attention_back_kernel, len(extra[0]) if extra else 0, groups), pos, args, specs,
        [sds((length, 3 * groups * cols), BF)] + [share] * 2,
        [pl.BlockSpec((length, 3 * cols), lambda j, *_: (0, jnp.minimum(j, last)))] + [share_spec] * 2,
        (steps,), [], "attention_back", after,
    )


def input_back_kernel(starts, count, pos, *refs):
    grads, refs = refs[: len(starts)], refs[len(starts) :]
    own, partner, *far = refs[: 2 + 4 * len(starts)]
    x_ref, mid_ref, mod_ref, gain_ref, sums_m, te, *rest = refs[2 + 4 * len(starts) :]
    biases, (out_ref, row_ref, sums_ref, *fulls) = rest[:count], rest[count:]
    width = x_ref.shape[1]
    cols = HEADS_PER_STEP * HEAD_DIM

    @pl.when(pl.program_id(0) == 0)
    def _():
        for i, full in enumerate(fulls):
            place_groups(full, pos, own, partner, far[4 * i : 4 * i + 4], starts[i], cols)

    back = jnp.zeros(x_ref.shape, F32)
    for grad, full in zip(grads, fulls):
        back += mm(grad[...], full[...], NT)
    scale = mod_ref[:, width : 2 * width]
    gain = gain_ref[...]
    n, r = normed(x_ref[...].astype(F32))
    back_sum = column_sum(back * n)
    out_ref[...] = mid_ref[...] + norm_back(back, n, r, gain, scale)
    add_sums(sums_ref, (column_sum(back), back_sum * gain, back_sum * (1.0 + scale)))

    @pl.when(pl.program_id(0) == pl.num_programs(0) - 1)
    def _():
        w = width
        row_ref[:, : 2 * w] = sums_ref[:, : 2 * w].astype(BF)
        row_ref[:, 2 * w : 6 * w] = sums_m[:, : 4 * w].astype(BF)
        row_ref[:, 6 * w : 7 * w] = sums_ref[:, 2 * w :].astype(BF)
        row_ref[:, 7 * w : 9 * w] = sums_m[:, 4 * w :].astype(BF)
        at = 9 * w
        spans = [b.shape[1] // 4 for b in biases]
        for i in range(4):
            for b, span in zip(biases, spans):
                row_ref[:, at : at + span] = b[:, i * span : (i + 1) * span].astype(BF)
                at += span
        row_ref[:, at:] = te[...]


def input_back(pos, grads, starts, weights, x, mid, mod, gain, sums_m, te, biases, after):
    length, width = x.shape
    args = (*grads, *weights, x, mid, mod, gain, sums_m, te, *biases)
    split = {*range(len(grads))} | {len(grads) + len(weights), len(grads) + len(weights) + 1}
    specs = [rows_of(a.shape) if i in split else once(a.shape) for i, a in enumerate(args)]
    row = (1, 9 * width + sum(b.shape[1] for b in biases) + te.shape[1])
    return call(
        partial(input_back_kernel, starts, len(biases)), pos, args, specs,
        [sds(x.shape, F32), sds(row, BF)], [rows_of(x.shape), whole(row)], (length // ROWS,),
        [pltpu.VMEM((1, 3 * width), F32)] + [pltpu.VMEM((width, g.shape[1]), BF) for g in grads], "input_back", after,
    )


SMALL = 256


def ada_kernel(count, pos, pair, got, shard, *refs):
    parts, (sums_ref, keep_ref, send_ref, all_rows) = refs[:count], refs[count:]
    rows, width = shard.shape
    cond = 4 * rows
    at = parts[0].shape[1]
    fold = UNIT // rows
    te_at = pair.shape[1] - cond
    all_rows[0:2, :] = pair[...].astype(F32)
    all_rows[2:4, :] = got[...].astype(F32)
    sums_ref[:, :at] = sum(p[:UNIT, :].astype(F32) for p in parts).astype(BF)
    mods = all_rows[0:4, :width].astype(BF)
    te = all_rows[0:4, te_at:].astype(BF)
    lane = lax.broadcasted_iota(jnp.int32, (rows, cond), 1)
    pick = (lane == pos[0] * rows + lax.broadcasted_iota(jnp.int32, (rows, cond), 0)).astype(BF)
    te_own = mm(pick, te, NT).astype(BF)
    grad = mm(te_own, mods).astype(BF)
    part = width // fold
    for i in range(fold):
        sums_ref[i * rows : (i + 1) * rows, at : at + part] = grad[:, i * part : (i + 1) * part]
    at += part
    total = jnp.sum(all_rows[0:4, :te_at], axis=0, keepdims=True)
    sums_ref[:, at:] = jnp.zeros((UNIT, SMALL), BF)
    for i in range(te_at // SMALL):
        sums_ref[i : i + 1, at : at + SMALL] = total[:, i * SMALL : (i + 1) * SMALL].astype(BF)
    tg = mm(mods, shard[...], NT)
    keep_ref[...] = tg[0:2]
    send_ref[...] = tg[2:4]


def ada_part(pos, pair, got, shard, parts, after):
    rows, width = shard.shape
    out = (UNIT, parts[0].shape[1] + width * rows // UNIT + SMALL)
    args = (pair, got, shard, *parts)
    return call(
        partial(ada_kernel, len(parts)), pos, args, [once(a.shape) for a in args],
        [sds(out, BF), sds((2, rows), F32), sds((2, rows), F32)], [once(out), once((2, rows)), once((2, rows))], (1,),
        [pltpu.VMEM((4, pair.shape[1]), F32)], "ada_part", after,
    )


def unpack_kernel(plan, pos, *refs):
    half = UNIT // 2
    count = len(plan)
    outs = refs[2 * count :]
    for i, moves in enumerate(plan):
        for which, ref in enumerate(refs[2 * i : 2 * i + 2]):
            for out, row, col, at, width in moves:
                place = pos[1] ^ which
                if row is None:
                    outs[out][:, pl.ds(pl.multiple_of(place * width, 128), width)] = ref[:, at : at + width].astype(F32)
                    continue
                base = pl.multiple_of(row + place * half, half)
                outs[out][pl.ds(base, half), col : col + width] = ref[:, at : at + width].astype(F32)


def unpack(pos, plan, pairs, shapes, after):
    args = [a for pair in pairs for a in pair]
    return call(
        partial(unpack_kernel, plan), pos, args, [once(a.shape) for a in args],
        [sds(s, F32) for s in shapes], [once(s) for s in shapes], (1,), [], "unpack", after,
    )


def mlp_rest_kernel(units, span, pos, near, far, down_in, up_in, down, up):
    half = UNIT // 2
    width = down.shape[1]
    block, owner = pl.program_id(0), pl.program_id(1)
    for which, ref in enumerate((near, far)):
        place = pos[1] ^ which

        @pl.when(owner == 0)
        def _():
            for k in range(TILE // UNIT):
                base = pl.multiple_of(k * UNIT + place * half, half)
                at = pl.multiple_of((block * (TILE // UNIT) + k) * width, 128)
                down[pl.ds(base, half), :] = ref[:, pl.ds(at, width)].astype(F32)

        for k in range(units):
            base = pl.multiple_of(k * UNIT + place * half, half)
            at = pl.multiple_of(span // UNIT * width + (owner * units + k) * span + block * TILE, 128)
            up[pl.ds(base, half), :] = ref[:, pl.ds(at, TILE)].astype(F32)


def mlp_rest(pos, pair, down, up, start, span, after):
    afters = after if isinstance(after, tuple) else (after,)
    hidden, width = down.shape
    units = up.shape[0] // UNIT
    per, base = hidden // TILE, start // TILE
    anywhere = pl.BlockSpec(memory_space=pl.ANY)
    args = (*pair, down, up)
    return call(
        partial(mlp_rest_kernel, units, span), pos, args, [once(a.shape) for a in pair] + [anywhere] * 2,
        [sds(down.shape, F32), sds(up.shape, F32)],
        [
            pl.BlockSpec((TILE, width), lambda j, i, *_: (base + j, 0)),
            pl.BlockSpec((up.shape[0], TILE), lambda j, i, *_: (0, i * per + base + j)),
        ],
        (span // TILE, 4), [], "mlp_rest", afters, aliases={1 + len(afters) + 2: 0, 1 + len(afters) + 3: 1},
    )


def last_kernel(units, cols, ada_at, pos, near, far, qkv_in, qkv, ada, small):
    half = UNIT // 2
    part = pl.program_id(0)
    width = ada.shape[1] * ada.shape[0] // UNIT
    for which, ref in enumerate((near, far)):
        place = pos[1] ^ which
        for k in range(units):
            base = pl.multiple_of(k * UNIT + place * half, half)
            at = pl.multiple_of((3 * k + part) * cols, 128)
            qkv[pl.ds(base, half), :] = ref[:, pl.ds(at, cols)].astype(F32)

        @pl.when(part == 0)
        def _():
            ada[:, pl.ds(pl.multiple_of(place * width, 128), width)] = ref[:, ada_at : ada_at + width].astype(F32)
            small[pl.ds(pl.multiple_of(place * half, half), half), :] = ref[:, ada_at + width :].astype(F32)


def last_unpack(pos, pair, qkv, ada_shape, after):
    afters = after if isinstance(after, tuple) else (after,)
    quarter, wide = qkv.shape
    cols = HEADS_PER_STEP * HEAD_DIM
    units = quarter // UNIT
    small = (UNIT, SMALL)
    args = (*pair, qkv)
    return call(
        partial(last_kernel, units, cols, units * 3 * cols), pos, args,
        [once(a.shape) for a in pair] + [pl.BlockSpec(memory_space=pl.ANY)],
        [sds(qkv.shape, F32), sds(ada_shape, F32), sds(small, F32)],
        [pl.BlockSpec((quarter, cols), lambda i, *_: (0, i * (wide // 3 // cols))), whole(ada_shape), whole(small)],
        (3,), [], "last_unpack", afters, aliases={1 + len(afters) + 2: 0},
    )


ORDER = ("g1", "F2", "MB", "g1", "g2", "Bb", "g1", "g2", "qb", "Ba", "g1", "g2", "qb", "qa", "IB", "g1", "qb", "g2", "row", "qa", "tg", "g1", "qb", "qa", "g2", "qb", "qa", "g2", "U1", "qb", "qa", "U2", "qa", "UB")
ENDS = {"U1": "g1", "U2": "g2", "UB": "qb"}
ROW_FIRST = {"g1": True, "g2": True, "qb": True}
WIDE_FIRST = True


def rotary_tables(length):
    half = HEAD_DIM // 2
    frequency = 10000.0 ** (-2.0 * np.arange(half) / HEAD_DIM)
    angles = np.arange(length)[:, None] * frequency[None, :]
    cos, sin = np.cos(angles), np.sin(angles)
    table = lambda *parts: jnp.asarray(np.concatenate(parts, axis=1).astype(np.float32))
    return table(cos, cos, cos, cos), table(-sin, sin, -sin, sin)


def local(
    mesh, block_input, cotangent, time_embed, ada_weight, ada_bias, attn_gain, qkv_weight, out_weight,
    mlp_gain, up_weight, up_bias, down_weight, down_bias,
):
    net = Net(mesh)
    length, width = block_input.shape
    f = net.f
    pos = jnp.stack([f] + [(net.d // bit) % 2 for bit in bits_of(net.dp)]).astype(jnp.int32)
    cond = time_embed.shape[1]
    quarter = width // 4
    ada_rows = ada_weight.shape[0]
    hidden_quarter = down_weight.shape[0]
    third = hidden_quarter // 3
    start_1, one = (0, 2 * third) if WIDE_FIRST else (2 * third, third)
    start_2, two = (2 * third, third) if WIDE_FIRST else (0, 2 * third)
    cols = HEADS_PER_STEP * HEAD_DIM
    groups = width // cols
    w = width
    cos, sin = rotary_tables(length)
    by_seq = lambda rel: jnp.take(rel, jnp.arange(4) ^ f, axis=0)

    units = quarter // UNIT
    in_groups = lambda a, b: [
        (0, k * UNIT, part * w + j * cols, cols) for k in range(units) for j in range(a, b) for part in range(3)
    ]
    of_up = lambda start, size: [
        (0, k * UNIT, i * hidden_quarter + start, size) for k in range(units) for i in range(4)
    ]
    of_down = lambda start, size: [(2, start + k * UNIT, 0, w) for k in range(size // UNIT)]
    rows = lambda v, at, n: lax.dynamic_slice_in_dim(v, at, n, 0)
    far_of = lambda near, far: (near, far, net.core_swap(near), net.core_swap(far))

    te_got = net.core_swap(time_embed)
    half_a, half_b = pack_halves(pos, [in_groups(0, 1), in_groups(1, groups)], [qkv_weight])
    half_a, attn_gain = tie(half_a, attn_gain)
    te = jnp.concatenate([time_embed, te_got], axis=0)
    te, half_b, attn_gain = tie(te, half_b, attn_gain)
    smalls = (attn_gain, mlp_gain, down_bias, up_bias, ada_bias)
    small = jnp.concatenate(smalls).reshape(1, -1)
    small_got = net.core_swap(small)
    te = jnp.concatenate([te, net.row_swap(te)], axis=0)
    near_a = net.row_swap(half_a)
    part = jnp.dot(
        lax.dynamic_slice_in_dim(by_seq(te), f * ada_rows, ada_rows, 1), ada_weight, preferred_element_type=F32
    )
    part_send = rows(part, 2 * (1 - net.row), 2)
    part_got = net.row_swap(part_send)
    small = jnp.concatenate([small, small_got], axis=0)
    small_far = net.row_swap(small)
    near_b = net.row_swap(half_b)
    partner_qkv = net.core_swap(qkv_weight)
    far_a = net.dp_swap(near_a, 1)
    up_weight, out_weight, down_weight, part_send = tie(up_weight, out_weight, down_weight, part_send)
    half_1, half_2, half_3 = pack_halves(
        pos,
        [
            of_up(start_1, one) + [(1, k * UNIT, 0, w) for k in range(units)], of_down(start_1, one),
            of_up(start_2, two) + of_down(start_2, two),
        ],
        [up_weight, out_weight, down_weight],
    )
    far_a = far_of(near_a, far_a)
    small = by_seq(jnp.concatenate([small, small_far], axis=0))
    part = rows(part, 2 * net.row, 2) + part_got
    cuts = np.cumsum([0] + [v.shape[0] for v in smalls])
    gain_a, gain_m, bias_d, bias_u, bias_ada = (
        small[:, cuts[i] : cuts[i + 1]].astype(F32).reshape(1, -1) for i in range(5)
    )
    mod = rows(part, net.core, 1) + net.core_swap(rows(part, 1 - net.core, 1)) + bias_ada
    near_b, block_input = tie(near_b, block_input)
    far_b = net.dp_swap(near_b, 1)
    near_1, near_2, near_3 = (net.row_swap(v) for v in (half_1, half_2, half_3))
    partner_out, partner_up, partner_down = (net.core_swap(v) for v in (out_weight, up_weight, down_weight))

    attn_in, *saved_a = attention_forward(
        pos, 0, 1, True, block_input, gain_a, mod, (qkv_weight, partner_qkv, *far_a), cos, sin
    )
    far_b, near_1, attn_in = tie(far_b, near_1, attn_in)
    far_b = far_of(near_b, far_b)
    far_1 = net.dp_swap(near_1, 1)
    saved_b = attention_forward(
        pos, 1, groups - 1, False, attn_in, gain_a, mod, (qkv_weight, partner_qkv, *far_b), cos, sin
    )
    if WIDE_FIRST:
        far_1, near_2, o_b = tie(far_1, near_2, saved_b[4])
    else:
        far_1, near_2, near_3, o_b = tie(far_1, near_2, near_3, saved_b[4])
    far_1 = far_of(near_1, far_1)
    far_2 = net.dp_swap(near_2, 1)
    os = (saved_a[4], o_b)
    branch, middle, mlp_in, mlp_grad, out_full = middle_forward(
        pos, os, block_input, cotangent, mod, gain_m, out_weight, partner_out, far_1, units * 4 * one
    )
    far_2, near_3, mlp_in = tie(far_2, near_3, mlp_in)
    far_2 = far_of(near_2, far_2)
    far_3 = net.dp_swap(near_3, 1)
    mb, back, bias_g1, *s1 = mlp(
        pos, mlp_in, mlp_grad, bias_u, (up_weight, partner_up, *far_1), (down_weight, partner_down, *far_2), 0,
        start_1, one, None, True,
    )
    far_3, mb, *s1 = tie(far_3, mb, *s1)
    far_3 = far_of(near_3, far_3)
    chunks = {"g1": Chunk(net, s1, ROW_FIRST["g1"])}
    state = {}

    def run(name, after):
        if name == "F2":
            mb2, back2, state["bias_g2"], *s2 = mlp(
                pos, mlp_in, mlp_grad, bias_u, (up_weight, partner_up, *far_3), (down_weight, partner_down, *far_3),
                units * 4 * two, start_2, two, (mb, back), True, after,
            )
            chunks["g2"] = Chunk(net, s2, ROW_FIRST["g2"])
            state["mb"], state["back"] = mb2, back2
            return back2
        if name == "MB":
            state["mid"], state["out"], state["low"], state["do"], state["sums_m"] = middle_back(
                pos, state["back"], state["mb"], middle, branch, cotangent, mod, gain_m, bias_d, out_full, after
            )
            return state["do"]
        if name == "Bb":
            state["grad_b"], *sb = attention_back(
                pos, saved_b, state["do"], cols, attn_in, cos, sin, (os, state["low"]), after
            )
            chunks["qb"] = Chunk(net, sb, ROW_FIRST["qb"])
            return state["grad_b"]
        if name == "Ba":
            state["grad_a"], *sa = attention_back(pos, saved_a, state["do"], 0, attn_in, cos, sin, None, after)
            chunks["qa"] = Chunk(net, sa, True, extend)
            return state["grad_a"]
        if name == "IB":
            state["input_grad"], row = input_back(
                pos, (state["grad_a"], state["grad_b"]), (0, 1), (qkv_weight, partner_qkv, *far_a, *far_b),
                block_input, state["mid"], mod, gain_a, state["sums_m"], time_embed, (bias_g1, state["bias_g2"]) if WIDE_FIRST else (state["bias_g2"], bias_g1), after,
            )
            state["row"], state["row_got"] = row, net.core_swap(row)
            return state["input_grad"]
        if name == "row":
            state["pair"] = jnp.concatenate([*follow(after, state["row"]), state["row_got"]], axis=0)
            state["pair_got"] = net.row_swap(state["pair"])
            return state["pair"]
        if name == "tg":
            keep, = follow(after, state["tg_keep"])
            state["give"] = jnp.concatenate([keep[1:2], state["tg_got"][1:2]], axis=0)
            state["given"] = net.core_swap(state["give"])
            return state["give"]
        if name == "U1":
            plan = [(0, start_1 + k * UNIT, 0, k * w, w) for k in range(one // UNIT)] + [
                (1, k * UNIT, i * hidden_quarter + start_1, one // UNIT * w + (i * units + k) * one, one)
                for i in range(4) for k in range(units)
            ]
            state["down_grad"], state["up_grad"] = unpack(
                pos, [plan], [chunks["g1"].ready], ((hidden_quarter, w), (quarter, 4 * hidden_quarter)), after
            )
            return state["up_grad"]
        if name == "UB":
            wide = units * 3 * cols
            plan = [
                (0, k * UNIT, part_ * w + j * cols, (j - 1) * wide + k * 3 * cols + part_ * cols, cols)
                for j in range(1, groups) for k in range(units) for part_ in range(3)
            ] + [(1, k * UNIT, 0, (groups - 1) * wide + k * w, w) for k in range(units)]
            state["qkv_grad"], state["out_grad"] = unpack(
                pos, [plan], [chunks["qb"].ready], ((quarter, 3 * w), (quarter, w)), after
            )
            return state["out_grad"]
        if name == "U2":
            state["down_grad"], state["up_grad"] = mlp_rest(
                pos, chunks["g2"].ready, state["down_grad"], state["up_grad"], start_2, two, after
            )
            return state["up_grad"]
        return chunks[name].step(after)

    def extend(parts, after):
        merged, state["tg_keep"], state["tg_send"] = ada_part(
            pos, state["pair"], state["pair_got"], ada_weight, [p.base for p in parts], after
        )
        state["tg_got"] = net.row_swap(state["tg_send"])
        return merged

    def finish(names, after):
        while any(chunks[n].where != "end" for n in names):
            for n in names:
                if chunks[n].where != "end":
                    after = run(n, after)
        return after

    after = None
    for name in ORDER:
        if name in chunks and chunks[name].where == "end":
            continue
        if name in ENDS:
            after = finish([ENDS[name]], after)
        after = run(name, after)
    after = finish(["qa"], after)

    block_output, input_grad = state["out"], state["input_grad"]
    down_grad, up_grad = state["down_grad"], state["up_grad"]
    qkv_grad, ada_weight_grad, small_sums = last_unpack(
        pos, chunks["qa"].ready, state["qkv_grad"], ada_weight.shape, after
    )
    out_grad = state["out_grad"]
    total = small_sums.reshape(-1)
    own_cols = lambda start, size: lax.dynamic_slice_in_dim(total, start + f * size, size, 0)
    ada_bias_grad = own_cols(0, 6 * w // 4)
    attn_gain_grad = own_cols(6 * w, quarter)
    mlp_gain_grad = own_cols(7 * w, quarter)
    down_bias_grad = own_cols(8 * w, quarter)
    up_bias_grad = own_cols(9 * w, up_bias.shape[0])
    tg_keep, tg_got, given = state["tg_keep"], state["tg_got"], state["given"]
    parts = jnp.concatenate([tg_keep[0:1], given[0:1], tg_got[0:1], given[1:2]], axis=0)
    time_grad = by_seq(parts).reshape(1, cond)
    return (
        block_output, input_grad, time_grad, ada_weight_grad, ada_bias_grad, attn_gain_grad, qkv_grad, out_grad,
        mlp_gain_grad, up_grad, up_bias_grad, down_grad, down_bias_grad,
    )


def solution(mesh):
    rows, shard, line = P(("dp", "fsdp"), None), P("fsdp", None), P("fsdp")
    return jax.shard_map(
        partial(local, mesh),
        mesh=mesh,
        in_specs=(rows, rows, rows, shard, line, line, shard, shard, line, shard, line, shard, line),
        out_specs=(rows, rows, rows, shard, line, line, shard, shard, line, shard, line, shard, line),
        check_vma=False,
    )
```
